32 devices in a mesh: rows: 16 (over z, y, x), rep: 2 (over core).
Axes of the slice: x: 2, y: 2, z: 4, core: 2. Of those that a mesh axis runs over, the one named last changes fastest.
Arguments:
- features: bfloat16 [4096, 256], P(('rows', 'rep')), may hold values from -6 to 6
- weight: bfloat16 [256, 256], replicated, may hold values from -0.375 to 0.375
- adj_tiles: bfloat16 [32, 2, 10, 128, 128], P('rows', 'rep'), may hold values from -0.25 to 0.25
- tile_cols: int32 [32, 2, 10], P('rows', 'rep'), may hold values from 0 to 15
- tile_counts: int32 [32, 2], P('rows', 'rep'), may hold values from 1 to 10, as said below
- out_grad: bfloat16 [4096, 256], P(('rows', 'rep')), may hold values from -6 to 6
- train_mask: int32 [4096], P(('rows', 'rep')), may hold values 0 or 1
Outputs:
- activations: bfloat16 [4096, 256], P(('rows', 'rep'))
- feat_grad: bfloat16 [4096, 256], P(('rows', 'rep'))
- weight_step: float32 [256, 256], replicated
The draws below stay inside these ranges and needn't reach their ends.
Inputs may be any that keep to these rules, and one draw needn't show every extreme that they name: Only the first tile_counts slots of a tile row are used; some tile row has all 10 slots live. `tile_cols`: columns may repeat within a tile row.
All inputs are finite; a program needn't handle non-finite values. No bound on the sum of `train_mask` on one device may be relied on, other than what follows from the above.
Results may differ from the reference program's by a relative error of at most 0.0062.
Values may be sent and summed in bfloat16 or wider, within the bound.
A program may use at most 64 MiB of HBM per device.

```python
import jax
import jax.numpy as jnp
from jax import lax

D = 256
TILE = 128
K = 10
NODE_DEV = 128
TR_ALL = 32
TC = 16
NODES = 4096
N_ROWS = 16
N_REP = 2


def draw_tile_counts(key, part):
    first_key, second_key = jax.random.split(jax.random.fold_in(key, 17))
    base_counts = jax.random.randint(first_key, (TR_ALL * N_REP,), 1, K + 1)
    full_spot = jax.random.randint(second_key, (), 0, TR_ALL * N_REP)
    positions = jnp.arange(TR_ALL * N_REP, dtype=jnp.int32)
    counts_flat = jnp.where(positions == full_spot, K, base_counts)
    return counts_flat.reshape(TR_ALL, N_REP).astype(jnp.int32)


def plant(values, own_key, least, top_value):
    index_at = [jax.random.randint(jax.random.fold_in(own_key, axis), (), 0, length) for axis, length in enumerate(values.shape)]
    widest = values.shape.index(max(values.shape))
    neighbour = index_at[:widest] + [(index_at[widest] + 1) % values.shape[widest]] + index_at[widest + 1:]
    return values.at[tuple(index_at)].set(least).at[tuple(neighbour)].set(top_value)


def level_of(key, extent, cuts, low, top_value):
    def one(position, shards_of):
        steps = jax.random.uniform(jax.random.fold_in(jax.random.fold_in(key, 6), position), (shards_of,), jnp.float32, low / len(cuts), top_value / len(cuts))
        return jnp.repeat(jnp.exp(steps), extent[position] // shards_of).reshape((-1,) + (1,) * (len(extent) - position - 1))

    gain = one(*cuts[0])
    for cut in cuts[1:]:
        gain = gain * one(*cut)
    return gain


def noise(own_key, dims, scale, most, pieces=(), kind=jnp.bfloat16):
    entries = scale * jax.random.normal(own_key, dims, jnp.float32)
    if pieces:
        entries = entries * level_of(own_key, dims, pieces, -0.22, 0.18)
    return jnp.clip(entries, -most, most).astype(kind)


def setup_inputs(seed: int = 0) -> dict:
    streams_of = jax.random.split(jax.random.key(seed), 8)
    return {
        "features": noise(streams_of[0], (NODES, D), 1.0, 6.0, ((0, 32),)),
        "weight": noise(streams_of[1], (D, D), D ** -0.5, 0.375),
        "adj_tiles": noise(streams_of[2], (TR_ALL, N_REP, K, TILE, TILE), (TILE * K // 2) ** -0.5, 0.25, ((0, 16), (1, 2))),
        "tile_cols": plant(jax.random.randint(streams_of[3], (TR_ALL, N_REP, K), 0, TC), jax.random.fold_in(streams_of[3], 1), 0, TC - 1).astype(jnp.int32),
        "tile_counts": draw_tile_counts(jax.random.fold_in(streams_of[7], 71), 0),
        "out_grad": noise(streams_of[5], (NODES, D), 1.0, 6.0, ((0, 32),)),
        "train_mask": plant((jax.random.randint(streams_of[6], (NODES,), 0, 4) < 1).astype(jnp.int32), jax.random.fold_in(streams_of[6], 1), 0, 1),
    }


def reference(features, weight, adj_tiles, tile_cols, tile_counts, out_grad, train_mask):
    group_feat = features.reshape(N_ROWS, N_REP, NODE_DEV, D).transpose(1, 0, 2, 3).reshape(N_REP, TC, TILE, D)
    live_mask = (jnp.arange(K, dtype=jnp.int32)[None, None, :] < tile_counts[:, :, None]).astype(jnp.float32)
    group_index = jnp.arange(N_REP, dtype=jnp.int32)[:, None]
    tile_index = jnp.arange(TR_ALL, dtype=jnp.int32)

    def forward_row(tile_row):
        adj_block = adj_tiles[tile_row].astype(jnp.float32) * live_mask[tile_row][:, :, None, None]
        picked = group_feat[group_index, tile_cols[tile_row]].astype(jnp.float32)
        return jnp.einsum('jkab,jkbd->ad', adj_block, picked)
    aggregated = lax.map(forward_row, tile_index).reshape(NODES, D).astype(jnp.bfloat16)
    pre_act = jnp.dot(aggregated, weight, preferred_element_type=jnp.float32)
    activations = jax.nn.silu(pre_act).astype(jnp.bfloat16)
    sigmoid_y = jax.nn.sigmoid(pre_act)
    silu_slope = sigmoid_y * (1.0 + pre_act * (1.0 - sigmoid_y))
    pre_grad = (out_grad.astype(jnp.float32) * train_mask.astype(jnp.float32)[:, None] * silu_slope).astype(jnp.bfloat16)
    wsum = lax.dot_general(aggregated, pre_grad, (((0,), (0,)), ((), ())), preferred_element_type=jnp.float32)
    weight_step = wsum / jnp.sqrt(jnp.mean(wsum * wsum) + 1e-06)
    agg_grad = lax.dot_general(pre_grad, weight, (((1,), (1,)), ((), ())), preferred_element_type=jnp.float32).astype(jnp.bfloat16)

    def backward_row(carry, tile_row):
        adj_block = adj_tiles[tile_row].astype(jnp.float32) * live_mask[tile_row][:, :, None, None]
        row_grads = lax.dynamic_slice_in_dim(agg_grad, tile_row * TILE, TILE, 0).astype(jnp.float32)
        contrib = jnp.einsum('jkab,ad->jkbd', adj_block, row_grads)
        carry = carry.at[group_index, tile_cols[tile_row]].add(contrib)
        return (carry, None)
    start_grad = jnp.zeros((N_REP, TC, TILE, D), jnp.float32)
    group_grad, unused_out = lax.scan(backward_row, start_grad, tile_index)
    feat_grad = group_grad.reshape(N_REP, N_ROWS, NODE_DEV, D).transpose(1, 0, 2, 3).reshape(NODES, D).astype(jnp.bfloat16)
    return (activations, feat_grad, weight_step)
```

```python
import functools

import jax
import jax.numpy as jnp
from jax import lax
from jax.experimental import pallas as pl
from jax.experimental.pallas import tpu as pltpu
from jax.sharding import PartitionSpec as P

MESH = pl.DeviceIdType.MESH
F32 = jnp.float32
BF16 = jnp.bfloat16
INNER = 4


def layer_kernel(
    n_rows, n_rep,
    feat_hbm, weight_hbm, adj_hbm, cols_hbm, counts_hbm, grad_hbm, mask_hbm,
    act_hbm, fgrad_hbm, wstep_hbm,
    act_ref, fgrad_ref, wstep_ref, out_sem,
    cols_ref, counts_ref, weight_ref, adj_ref, grad_ref, mask_ref,
    panel, dense, dense_t, masked, acc, part_in, shared,
    w_full, w_out, w_in, w_all, terms, own_plane, in_part, in_far, in_own, in_z,
    load_sem, ag_send, ag_recv, masked_send, masked_recv, part_send, part_recv, grads_send, grads_recv,
    w_send, w_recv, wa_send, wa_recv, swap_send, swap_recv,
    rs_send, in_part_recv, in_far_recv, in_own_recv, in_z_recv,
):
    nodes, width = feat_hbm.shape
    tile_rows, slots, tile = adj_ref.shape[0], adj_ref.shape[2], adj_ref.shape[3]
    piece = w_out.shape[1]
    half = w_out.shape[2]
    outer_count = n_rows // INNER
    both = n_rep == 2
    block_rows = n_rep * nodes
    plane_nodes = INNER * nodes
    row = lax.axis_index("rows")
    rep = lax.axis_index("rep")
    outer, inner = row // INNER, row % INNER
    iy, ix = inner // 2, inner % 2
    inner_x, inner_y = iy * 2 + (1 - ix), (1 - iy) * 2 + ix
    inner_d = (1 - iy) * 2 + (1 - ix)
    side_of = outer % 2
    partner = outer + 1 - 2 * side_of
    pair, pairs = outer // 2, outer_count // 2
    others = [(pair + d) % pairs for d in range(1, pairs)]
    far_gather = [2 * q + m for q in others for m in (1 - side_of, side_of)]
    far_reduce = [2 * q + m for q in others[::-1] for m in (side_of, 1 - side_of)]
    rep_peers = [(rep + d) % n_rep for d in range(1, n_rep)]
    row_peers = [(row + d) % n_rows for d in range(1, n_rows)]
    plane_inners = (inner_d, inner_x, inner_y)
    pending = []
    store_act, store_fgrad, store_wstep = [
        pltpu.make_async_copy(src, dst, out_sem.at[n])
        for n, (src, dst) in enumerate([(act_ref, act_hbm), (fgrad_ref, fgrad_hbm), (wstep_ref, wstep_hbm)])
    ]

    def remote(src, dst, send, recv, row_to, rep_to):
        return pltpu.make_async_remote_copy(
            src_ref=src, dst_ref=dst, send_sem=send, recv_sem=recv,
            device_id=(row_to, rep_to), device_id_type=MESH,
        )

    def post(*spec):
        copy = remote(*spec)
        copy.start()
        pending.append(copy)

    def drain():
        while pending:
            pending.pop(0).wait_send()

    def at(o, i):
        return o * INNER + i

    barrier = pltpu.get_barrier_semaphore()
    near = [(at(o, inner), rep) for o in [partner] + far_gather]
    near += [(at(outer, i), rep) for i in plane_inners]
    near += [(row, p) for p in rep_peers]
    for other in near:
        pl.semaphore_signal(barrier, inc=1, device_id=other, device_id_type=MESH)
    loads = [
        pltpu.make_async_copy(src, dst, load_sem.at[n])
        for n, (src, dst) in enumerate([
            (adj_hbm, adj_ref), (cols_hbm, cols_ref), (counts_hbm, counts_ref),
            (grad_hbm, grad_ref), (mask_hbm, mask_ref), (feat_hbm, panel.at[row]),
            (weight_hbm, weight_ref),
        ])
    ]
    for load in loads:
        load.start()
    pl.semaphore_wait(barrier, len(near))

    gather_count = iter(range(n_rows))

    def gather(src, source, row_to):
        post(src, panel.at[source], ag_send.at[next(gather_count)], ag_recv.at[source], row_to, rep)

    def gathered(source):
        remote(
            panel.at[source], panel.at[source], ag_send.at[0], ag_recv.at[source],
            at(outer, inner_x), rep,
        ).wait_recv()

    for o in far_gather:
        gather(feat_hbm, row, at(o, inner))
    for i in plane_inners:
        gather(feat_hbm, row, at(outer, i))
    gather(feat_hbm, row, at(partner, inner))
    for load in loads[:5]:
        load.wait()

    def build(r, start, stop):
        def column(c, carry):
            total = jnp.zeros((tile, tile), F32)
            for k in range(slots):
                chosen = jnp.logical_and(cols_ref[r, 0, k] == c, k < counts_ref[r])
                total = total + jnp.where(chosen, 1.0, 0.0) * adj_ref[r, 0, k].astype(F32)
            place = pl.multiple_of(c * tile, tile)
            dense[r * tile:(r + 1) * tile, pl.ds(place, tile)] = total.astype(BF16)
            dense_t[pl.ds(place, tile), r * tile:(r + 1) * tile] = total.T.astype(BF16)
            return carry

        lax.fori_loop(start, stop, column, 0)

    stride = n_rows // 8
    jobs = [(r, c, c + stride) for r in range(tile_rows) for c in range(0, n_rows, stride)]

    def build_jobs(count):
        for _ in range(min(count, len(jobs))):
            build(*jobs.pop(0))

    mask_col = jnp.broadcast_to(mask_ref[...].astype(F32), (nodes, nodes)).T
    mask = jnp.concatenate([mask_col] * (width // nodes), axis=1)
    masked[rep] = (grad_ref[...].astype(F32) * mask).astype(BF16)
    if both:
        for p in rep_peers:
            post(masked.at[rep], masked.at[rep], masked_send, masked_recv, row, p)

    def to_partner(i):
        gathered(at(outer, i))
        gather(panel.at[at(outer, i)], at(outer, i), at(partner, inner))

    def to_plane(o):
        gathered(at(o, inner))
        for i in plane_inners:
            gather(panel.at[at(o, inner)], at(o, inner), at(outer, i))

    share = len(jobs)
    build_jobs(share * 3 // 8)
    to_partner(inner_x)
    to_partner(inner_y)
    for n, o in enumerate(far_gather):
        build_jobs(max(1, share // (4 * len(far_gather))) if n == 0 else max(1, share // (2 * len(far_gather))))
        to_plane(o)
        if n == 0:
            to_partner(inner_d)
    build_jobs(len(jobs))
    for load in loads[5:]:
        load.wait()

    def product(o, rows_at):
        place = pl.multiple_of(o * plane_nodes, plane_nodes)
        planes = panel[pl.ds(pl.multiple_of(o * INNER, INNER), INNER)].reshape(plane_nodes, width)
        return jnp.dot(dense[rows_at, pl.ds(place, plane_nodes)], planes, preferred_element_type=F32)

    everything = pl.ds(0, block_rows)
    order = [outer] + far_gather[:-1] + [partner] + far_gather[-1:]
    for n, o in enumerate(order[:-1]):
        if n > 0:
            for i in plane_inners + ((inner,) if n == len(order) - 2 else ()):
                gathered(at(o, i))
        value = product(o, everything)
        acc[...] = value if n == 0 else acc[...] + value
    last = order[-1]
    for i in plane_inners:
        gathered(at(last, i))

    def rows_of(p):
        return pl.ds(p * nodes if isinstance(p, int) else pl.multiple_of(p * nodes, nodes), nodes)

    def finish_product(p):
        acc[rows_of(p), :] = acc[rows_of(p), :] + product(last, rows_of(p))

    def slope_of(pre_act, sigmoid):
        return sigmoid * (1.0 + pre_act * (1.0 - sigmoid))

    if both:
        other = rep_peers[0]
        for r in range(n_rep):
            finish_product(r)
            post(acc.at[rows_of(r)], part_in.at[r], part_send.at[r], part_recv.at[r], row, other)
        remote(masked.at[rep], masked.at[other], masked_send, masked_recv, row, other).wait_recv()
        for r in range(n_rep):
            remote(acc.at[rows_of(r)], part_in.at[r], part_send.at[r], part_recv.at[r], row, other).wait_recv()
            aggregated = (acc[rows_of(r), :] + part_in[r]).astype(BF16)
            shared[0, r] = aggregated
            pre_act = jnp.dot(aggregated, weight_ref[...], preferred_element_type=F32)
            sigmoid = jax.nn.sigmoid(pre_act)
            shared[1, r] = (masked[r].astype(F32) * slope_of(pre_act, sigmoid)).astype(BF16)

            @pl.when(rep == r)
            def _():
                act_ref[...] = (pre_act * sigmoid).astype(BF16)
    else:
        for d, p in enumerate(rep_peers):
            finish_product(p)
            post(acc.at[rows_of(p)], part_in.at[rep], part_send.at[d], part_recv.at[rep], row, p)
        finish_product(rep)
        total = acc[rows_of(rep), :]
        for p in rep_peers:
            remote(acc.at[rows_of(p)], part_in.at[p], part_send.at[0], part_recv.at[p], row, p).wait_recv()
            total = total + part_in[p]
        aggregated = total.astype(BF16)
        shared[0, rep] = aggregated
        for d, p in enumerate(rep_peers):
            post(shared.at[0, rep], shared.at[0, rep], grads_send.at[0, d], grads_recv.at[0, rep], row, p)
        pre_act = jnp.dot(aggregated, weight_ref[...], preferred_element_type=F32)
        sigmoid = jax.nn.sigmoid(pre_act)
        shared[1, rep] = (masked[rep].astype(F32) * slope_of(pre_act, sigmoid)).astype(BF16)
        for d, p in enumerate(rep_peers):
            post(shared.at[1, rep], shared.at[1, rep], grads_send.at[1, d], grads_recv.at[1, rep], row, p)
        act_ref[...] = (pre_act * sigmoid).astype(BF16)
        for n in range(2):
            for p in rep_peers:
                remote(shared.at[n, p], shared.at[n, p], grads_send.at[0, 0], grads_recv.at[n, p], row, p).wait_recv()

    store_act.start()
    row_pre_grads = shared[1].reshape(block_rows, width)
    row_grads = lax.dot_general(
        row_pre_grads, weight_ref[...], (((1,), (1,)), ((), ())), preferred_element_type=F32
    ).astype(BF16)

    def w_send_terms():
        column = pl.multiple_of((rep % 2) * half, half)
        w_full[...] = lax.dot_general(
            shared[0].reshape(block_rows, width), row_pre_grads,
            (((0,), (0,)), ((), ())), preferred_element_type=F32,
        )
        w_half = w_full[:, pl.ds(column, half)]
        for b in range(n_rows):
            w_out[b] = w_half[b * piece:(b + 1) * piece].astype(w_out.dtype)
        for n, to in enumerate(row_peers):
            post(w_out.at[to], w_in.at[row], w_send.at[n], w_recv.at[row], to, rep)
        w_in[row] = w_out[row]

    def w_send_sums():
        for to in row_peers:
            remote(w_out.at[to], w_in.at[to], w_send.at[0], w_recv.at[to], to, rep).wait_recv()
        side = rep % 2
        w_all[side, row] = jnp.sum(w_in[...].astype(F32), axis=0).astype(w_all.dtype)
        for n, to in enumerate(row_peers):
            post(w_all.at[side, row], w_all.at[side, row], wa_send.at[n], wa_recv.at[row], to, rep)

    def w_swap():
        side = rep % 2
        for to in row_peers:
            block = w_all.at[side, to]
            remote(block, block, wa_send.at[0], wa_recv.at[to], to, rep).wait_recv()
        post(w_all.at[side], w_all.at[side], swap_send, swap_recv, row, (rep + 1) % n_rep)

    def w_finish():
        other_side = w_all.at[(rep + 1) % 2]
        remote(other_side, other_side, swap_send, swap_recv, row, (rep + 1) % n_rep).wait_recv()
        whole = w_all[...].astype(F32)
        scale = lax.rsqrt(jnp.sum(whole * whole) / (width * width) + 1e-06)
        for side in range(2):
            for b in range(n_rows):
                wstep_ref[b * piece:(b + 1) * piece, side * half:(side + 1) * half] = whole[side, b] * scale

    def plane_product(o):
        place = pl.multiple_of(o * plane_nodes, plane_nodes)
        value = jnp.dot(dense_t[pl.ds(place, plane_nodes), :], row_grads, preferred_element_type=F32)
        return value.reshape(INNER, nodes, width)

    reduce_count = iter(range(n_rows))

    def give(src, dst, recv, row_to):
        post(src, dst, rs_send.at[next(reduce_count)], recv, row_to, rep)

    def taken(dst, recv):
        remote(dst, dst, rs_send.at[0], recv, at(outer, inner_x), rep).wait_recv()

    def far_terms(o):
        terms[pl.ds(pl.multiple_of(o * INNER, INNER), INNER)] = plane_product(o).astype(BF16)
        for i in plane_inners:
            give(terms.at[at(o, i)], in_far.at[o, inner], in_far_recv.at[o, inner], at(outer, i))

    def partner_terms():
        terms[pl.ds(pl.multiple_of(partner * INNER, INNER), INNER)] = plane_product(partner).astype(BF16)
        for i in plane_inners + (inner,):
            give(terms.at[at(partner, i)], in_part.at[i], in_part_recv.at[i], at(partner, inner))

    def plane_sum(i):
        taken(in_part.at[i], in_part_recv.at[i])
        c = at(outer, i)
        terms[c] = (own_plane[i] + in_part[i].astype(F32)).astype(BF16)
        give(terms.at[c], in_own.at[inner], in_own_recv.at[inner], c)

    def far_sum(o):
        c = at(o, inner)
        total = terms[c].astype(F32)
        for i in plane_inners:
            taken(in_far.at[o, i], in_far_recv.at[o, i])
            total = total + in_far[o, i].astype(F32)
        terms[c] = total.astype(BF16)
        give(terms.at[c], in_z.at[outer], in_z_recv.at[outer], c)

    w_send_terms()
    for n, o in enumerate(far_reduce):
        far_terms(o)
        if n == 0:
            partner_terms()
    if not far_reduce:
        partner_terms()
    own_plane[...] = plane_product(outer)
    plane_sum(inner_d)
    for n, o in enumerate(far_reduce):
        far_sum(o)
        if n == 0:
            w_send_sums()
            plane_sum(inner_x)
            plane_sum(inner_y)
    w_swap()
    drain()
    w_finish()
    store_wstep.start()
    taken(in_part.at[inner], in_part_recv.at[inner])
    total = own_plane[inner] + in_part[inner].astype(F32)
    for i in plane_inners:
        taken(in_own.at[i], in_own_recv.at[i])
        total = total + in_own[i].astype(F32)
    for o in far_reduce:
        taken(in_z.at[o], in_z_recv.at[o])
        total = total + in_z[o].astype(F32)
    fgrad_ref[...] = total.astype(BF16)
    store_fgrad.start()
    drain()
    for store in (store_act, store_wstep, store_fgrad):
        store.wait()


def result_kernel(act_in, fgrad_in, wstep_in, act_hbm, fgrad_hbm, wstep_hbm, act_ref, fgrad_ref, wstep_ref, in_sem, out_sem):
    ins = [
        pltpu.make_async_copy(src, dst, in_sem.at[n])
        for n, (src, dst) in enumerate([(act_in, act_ref), (fgrad_in, fgrad_ref), (wstep_in, wstep_ref)])
    ]
    outs = [
        pltpu.make_async_copy(src, dst, out_sem.at[n])
        for n, (src, dst) in enumerate([(act_ref, act_hbm), (fgrad_ref, fgrad_hbm), (wstep_ref, wstep_hbm)])
    ]
    for copy in ins:
        copy.start()
    for copy_in, copy_out in zip(ins, outs):
        copy_in.wait()
        copy_out.start()
    for copy in outs:
        copy.wait()


def body(n_rows, n_rep, features, weight, adj_tiles, tile_cols, tile_counts, out_grad, train_mask):
    nodes, width = features.shape
    tile_rows, tile = adj_tiles.shape[0], adj_tiles.shape[-1]
    outer_count = n_rows // INNER
    piece = width // n_rows
    half = width // 2
    w_type = BF16 if piece % 16 == 0 else F32
    vmem = pl.BlockSpec(memory_space=pltpu.VMEM)
    hbm = pl.BlockSpec(memory_space=pltpu.HBM)
    dma = pltpu.SemaphoreType.DMA
    vmem_bytes = int((60 if n_rows <= 16 else 63) * 1024 * 1024)
    block = (nodes, width)
    outs = (
        jax.ShapeDtypeStruct(block, BF16),
        jax.ShapeDtypeStruct(block, BF16),
        jax.ShapeDtypeStruct((width, width), F32),
    )
    counts = tile_counts.reshape(-1)
    results = pl.pallas_call(
        functools.partial(layer_kernel, n_rows, n_rep),
        out_shape=outs,
        in_specs=[hbm] * 7,
        out_specs=(hbm, hbm, hbm),
        scratch_shapes=[
            pltpu.VMEM(block, BF16),
            pltpu.VMEM(block, BF16),
            pltpu.VMEM((width, width), F32),
            dma((3,)),
            pltpu.SMEM(tile_cols.shape, jnp.int32),
            pltpu.SMEM(counts.shape, jnp.int32),
            pltpu.VMEM(weight.shape, BF16),
            pltpu.VMEM(adj_tiles.shape, BF16),
            pltpu.VMEM(block, BF16),
            pltpu.VMEM((1, nodes), jnp.int32),
            pltpu.VMEM((n_rows,) + block, BF16),
            pltpu.VMEM((tile_rows * tile, n_rows * tile), BF16),
            pltpu.VMEM((n_rows * tile, tile_rows * tile), BF16),
            pltpu.VMEM((n_rep,) + block, BF16),
            pltpu.VMEM((n_rep * nodes, width), F32),
            pltpu.VMEM((n_rep,) + block, F32),
            pltpu.VMEM((2, n_rep) + block, BF16),
            pltpu.VMEM((width, width), F32),
            pltpu.VMEM((n_rows, piece, half), w_type),
            pltpu.VMEM((n_rows, piece, half), w_type),
            pltpu.VMEM((2, n_rows, piece, half), w_type),
            pltpu.VMEM((n_rows,) + block, BF16),
            pltpu.VMEM((INNER,) + block, F32),
            pltpu.VMEM((INNER,) + block, BF16),
            pltpu.VMEM((outer_count, INNER) + block, BF16),
            pltpu.VMEM((INNER,) + block, BF16),
            pltpu.VMEM((outer_count,) + block, BF16),
            dma((7,)),
            dma((n_rows,)), dma((n_rows,)),
            dma, dma,
            dma((n_rep,)), dma((n_rep,)),
            dma((2, n_rep)), dma((2, n_rep)),
            dma((n_rows,)), dma((n_rows,)),
            dma((n_rows,)), dma((n_rows,)),
            dma, dma,
            dma((n_rows,)), dma((INNER,)), dma((outer_count, INNER)), dma((INNER,)), dma((outer_count,)),
        ],
        compiler_params=pltpu.CompilerParams(
            collective_id=0, has_side_effects=True, vmem_limit_bytes=vmem_bytes
        ),
    )(
        features, weight, adj_tiles, tile_cols, counts, out_grad, train_mask.reshape(1, -1),
    )
    return pl.pallas_call(
        result_kernel,
        out_shape=outs,
        in_specs=[hbm] * 3,
        out_specs=(hbm, hbm, hbm),
        scratch_shapes=[pltpu.VMEM(block, BF16), pltpu.VMEM(block, BF16), pltpu.VMEM((width, width), F32), dma((3,)), dma((3,))],
    )(*results)


def solution(mesh):
    placed = (
        P(("rows", "rep"), None),
        P(),
        P("rows", "rep", None, None, None),
        P("rows", "rep", None),
        P("rows", "rep"),
        P(("rows", "rep"), None),
        P(("rows", "rep")),
    )
    return jax.shard_map(
        functools.partial(body, mesh.shape["rows"], mesh.shape["rep"]),
        mesh=mesh,
        in_specs=placed,
        out_specs=(P(("rows", "rep"), None), P(("rows", "rep"), None), P()),
        check_vma=False,
    )
```

```python
import functools

import jax
import jax.numpy as jnp
from jax import lax
from jax.experimental import pallas as pl
from jax.experimental.pallas import tpu as pltpu
from jax.sharding import PartitionSpec as P

MESH = pl.DeviceIdType.MESH
F32 = jnp.float32
BF16 = jnp.bfloat16
INNER = 4
PARTS = 4


def layer_kernel(
    n_rows, n_rep,
    feat_hbm, weight_hbm, adj_hbm, cols_hbm, counts_hbm, grad_hbm, mask_hbm,
    act_ref, fgrad_ref, wstep_0, wstep_1, wstep_2, wstep_3,
    cols_ref, counts_ref, weight_ref, adj_ref, grad_ref, mask_ref,
    panel, dense, dense_t, masked, acc, part_in, shared,
    w_full, w_out, w_in, w_all, terms, own_plane, in_part, in_far, in_own, in_z,
    load_sem, ag_send, ag_recv, masked_send, masked_recv, part_send, part_recv, grads_send, grads_recv,
    w_send, w_recv, wa_send, wa_recv, swap_send, swap_recv,
    rs_send, in_part_recv, in_far_recv, in_own_recv, in_z_recv,
):
    nodes, width = feat_hbm.shape
    tile_rows, slots, tile = adj_ref.shape[0], adj_ref.shape[2], adj_ref.shape[3]
    piece = w_out.shape[1]
    half = w_out.shape[2]
    outer_count = n_rows // INNER
    both = n_rep == 2
    block_rows = n_rep * nodes
    quarters = (wstep_0, wstep_1, wstep_2, wstep_3)
    plane_nodes = INNER * nodes
    row = lax.axis_index("rows")
    rep = lax.axis_index("rep")
    outer, inner = row // INNER, row % INNER
    iy, ix = inner // 2, inner % 2
    inner_x, inner_y = iy * 2 + (1 - ix), (1 - iy) * 2 + ix
    inner_d = (1 - iy) * 2 + (1 - ix)
    side_of = outer % 2
    partner = outer + 1 - 2 * side_of
    pair, pairs = outer // 2, outer_count // 2
    others = [(pair + d) % pairs for d in range(1, pairs)]
    far_gather = [2 * q + m for q in others for m in (1 - side_of, side_of)]
    far_reduce = [2 * q + m for q in others[::-1] for m in (side_of, 1 - side_of)]
    rep_peers = [(rep + d) % n_rep for d in range(1, n_rep)]
    row_peers = [(row + d) % n_rows for d in range(1, n_rows)]
    plane_inners = (inner_d, inner_x, inner_y)
    pending = []

    def remote(src, dst, send, recv, row_to, rep_to):
        return pltpu.make_async_remote_copy(
            src_ref=src, dst_ref=dst, send_sem=send, recv_sem=recv,
            device_id=(row_to, rep_to), device_id_type=MESH,
        )

    def post(*spec):
        copy = remote(*spec)
        copy.start()
        pending.append(copy)

    def drain():
        while pending:
            pending.pop(0).wait_send()

    def at(o, i):
        return o * INNER + i

    barrier = pltpu.get_barrier_semaphore()
    near = [(at(o, inner), rep) for o in [partner] + far_gather]
    near += [(at(outer, i), rep) for i in plane_inners]
    near += [(row, p) for p in rep_peers]
    for other in near:
        pl.semaphore_signal(barrier, inc=1, device_id=other, device_id_type=MESH)
    loads = [
        pltpu.make_async_copy(src, dst, load_sem.at[n])
        for n, (src, dst) in enumerate([
            (adj_hbm, adj_ref), (cols_hbm, cols_ref), (counts_hbm, counts_ref),
            (grad_hbm, grad_ref), (mask_hbm, mask_ref), (feat_hbm, panel.at[row]),
            (weight_hbm, weight_ref),
        ])
    ]
    for load in loads:
        load.start()
    pl.semaphore_wait(barrier, len(near))

    gather_count = iter(range(n_rows))

    def gather(src, source, row_to):
        post(src, panel.at[source], ag_send.at[next(gather_count)], ag_recv.at[source], row_to, rep)

    def gathered(source):
        remote(
            panel.at[source], panel.at[source], ag_send.at[0], ag_recv.at[source],
            at(outer, inner_x), rep,
        ).wait_recv()

    for o in far_gather:
        gather(feat_hbm, row, at(o, inner))
    for i in plane_inners:
        gather(feat_hbm, row, at(outer, i))
    gather(feat_hbm, row, at(partner, inner))
    for load in loads[:5]:
        load.wait()

    def build(r, start, stop):
        def column(c, carry):
            total = jnp.zeros((tile, tile), F32)
            for k in range(slots):
                chosen = jnp.logical_and(cols_ref[r, 0, k] == c, k < counts_ref[r])
                total = total + jnp.where(chosen, 1.0, 0.0) * adj_ref[r, 0, k].astype(F32)
            place = pl.multiple_of(c * tile, tile)
            dense[r * tile:(r + 1) * tile, pl.ds(place, tile)] = total.astype(BF16)
            dense_t[pl.ds(place, tile), r * tile:(r + 1) * tile] = total.T.astype(BF16)
            return carry

        lax.fori_loop(start, stop, column, 0)

    stride = n_rows // 8
    jobs = [(r, c, c + stride) for r in range(tile_rows) for c in range(0, n_rows, stride)]

    def build_jobs(count):
        for _ in range(min(count, len(jobs))):
            build(*jobs.pop(0))

    mask_col = jnp.broadcast_to(mask_ref[...].astype(F32), (nodes, nodes)).T
    mask = jnp.concatenate([mask_col] * (width // nodes), axis=1)
    masked[rep] = (grad_ref[...].astype(F32) * mask).astype(BF16)
    if both:
        for p in rep_peers:
            post(masked.at[rep], masked.at[rep], masked_send, masked_recv, row, p)

    def to_partner(i):
        gathered(at(outer, i))
        gather(panel.at[at(outer, i)], at(outer, i), at(partner, inner))

    def to_plane(o):
        gathered(at(o, inner))
        for i in plane_inners:
            gather(panel.at[at(o, inner)], at(o, inner), at(outer, i))

    share = len(jobs)
    build_jobs(share * 3 // 8)
    to_partner(inner_x)
    to_partner(inner_y)
    for n, o in enumerate(far_gather):
        build_jobs(max(1, share // (4 * len(far_gather))) if n == 0 else max(1, share // (2 * len(far_gather))))
        to_plane(o)
        if n == 0:
            to_partner(inner_d)
    build_jobs(len(jobs))
    for load in loads[5:]:
        load.wait()

    def product(o, rows_at):
        place = pl.multiple_of(o * plane_nodes, plane_nodes)
        planes = panel[pl.ds(pl.multiple_of(o * INNER, INNER), INNER)].reshape(plane_nodes, width)
        return jnp.dot(dense[rows_at, pl.ds(place, plane_nodes)], planes, preferred_element_type=F32)

    everything = pl.ds(0, block_rows)
    order = [outer] + far_gather[:-1] + [partner] + far_gather[-1:]
    for n, o in enumerate(order[:-1]):
        if n > 0:
            for i in plane_inners + ((inner,) if n == len(order) - 2 else ()):
                gathered(at(o, i))
        value = product(o, everything)
        acc[...] = value if n == 0 else acc[...] + value
    last = order[-1]
    for i in plane_inners:
        gathered(at(last, i))

    def rows_of(p):
        return pl.ds(p * nodes if isinstance(p, int) else pl.multiple_of(p * nodes, nodes), nodes)

    def finish_product(p):
        acc[rows_of(p), :] = acc[rows_of(p), :] + product(last, rows_of(p))

    def slope_of(pre_act, sigmoid):
        return sigmoid * (1.0 + pre_act * (1.0 - sigmoid))

    if both:
        other = rep_peers[0]
        for r in range(n_rep):
            finish_product(r)
            post(acc.at[rows_of(r)], part_in.at[r], part_send.at[r], part_recv.at[r], row, other)
        remote(masked.at[rep], masked.at[other], masked_send, masked_recv, row, other).wait_recv()
        for r in range(n_rep):
            remote(acc.at[rows_of(r)], part_in.at[r], part_send.at[r], part_recv.at[r], row, other).wait_recv()
            aggregated = (acc[rows_of(r), :] + part_in[r]).astype(BF16)
            shared[0, r] = aggregated
            pre_act = jnp.dot(aggregated, weight_ref[...], preferred_element_type=F32)
            sigmoid = jax.nn.sigmoid(pre_act)
            shared[1, r] = (masked[r].astype(F32) * slope_of(pre_act, sigmoid)).astype(BF16)

            @pl.when(rep == r)
            def _():
                act_ref[...] = (pre_act * sigmoid).astype(BF16)
    else:
        for d, p in enumerate(rep_peers):
            finish_product(p)
            post(acc.at[rows_of(p)], part_in.at[rep], part_send.at[d], part_recv.at[rep], row, p)
        finish_product(rep)
        total = acc[rows_of(rep), :]
        for p in rep_peers:
            remote(acc.at[rows_of(p)], part_in.at[p], part_send.at[0], part_recv.at[p], row, p).wait_recv()
            total = total + part_in[p]
        aggregated = total.astype(BF16)
        shared[0, rep] = aggregated
        for d, p in enumerate(rep_peers):
            post(shared.at[0, rep], shared.at[0, rep], grads_send.at[0, d], grads_recv.at[0, rep], row, p)
        pre_act = jnp.dot(aggregated, weight_ref[...], preferred_element_type=F32)
        sigmoid = jax.nn.sigmoid(pre_act)
        shared[1, rep] = (masked[rep].astype(F32) * slope_of(pre_act, sigmoid)).astype(BF16)
        for d, p in enumerate(rep_peers):
            post(shared.at[1, rep], shared.at[1, rep], grads_send.at[1, d], grads_recv.at[1, rep], row, p)
        act_ref[...] = (pre_act * sigmoid).astype(BF16)
        for n in range(2):
            for p in rep_peers:
                remote(shared.at[n, p], shared.at[n, p], grads_send.at[0, 0], grads_recv.at[n, p], row, p).wait_recv()

    row_pre_grads = shared[1].reshape(block_rows, width)
    row_grads = lax.dot_general(
        row_pre_grads, weight_ref[...], (((1,), (1,)), ((), ())), preferred_element_type=F32
    ).astype(BF16)

    def w_send_terms():
        column = pl.multiple_of((rep % 2) * half, half)
        w_full[...] = lax.dot_general(
            shared[0].reshape(block_rows, width), row_pre_grads,
            (((0,), (0,)), ((), ())), preferred_element_type=F32,
        )
        w_half = w_full[:, pl.ds(column, half)]
        for b in range(n_rows):
            w_out[b] = w_half[b * piece:(b + 1) * piece].astype(w_out.dtype)
        for n, to in enumerate(row_peers):
            post(w_out.at[to], w_in.at[row], w_send.at[n], w_recv.at[row], to, rep)
        w_in[row] = w_out[row]

    def w_send_sums():
        for to in row_peers:
            remote(w_out.at[to], w_in.at[to], w_send.at[0], w_recv.at[to], to, rep).wait_recv()
        side = rep % 2
        w_all[side, row] = jnp.sum(w_in[...].astype(F32), axis=0).astype(w_all.dtype)
        for n, to in enumerate(row_peers):
            post(w_all.at[side, row], w_all.at[side, row], wa_send.at[n], wa_recv.at[row], to, rep)

    def w_swap():
        side = rep % 2
        for to in row_peers:
            block = w_all.at[side, to]
            remote(block, block, wa_send.at[0], wa_recv.at[to], to, rep).wait_recv()
        post(w_all.at[side], w_all.at[side], swap_send, swap_recv, row, (rep + 1) % n_rep)

    def w_finish():
        other_side = w_all.at[(rep + 1) % 2]
        remote(other_side, other_side, swap_send, swap_recv, row, (rep + 1) % n_rep).wait_recv()
        whole = w_all[...].astype(F32)
        scale = lax.rsqrt(jnp.sum(whole * whole) / (width * width) + 1e-06)
        for side in range(2):
            for b in range(n_rows):
                ref, first = quarters[b * piece * PARTS // width], b * piece % (width // PARTS)
                ref[first:first + piece, side * half:(side + 1) * half] = whole[side, b] * scale

    def plane_product(o):
        place = pl.multiple_of(o * plane_nodes, plane_nodes)
        value = jnp.dot(dense_t[pl.ds(place, plane_nodes), :], row_grads, preferred_element_type=F32)
        return value.reshape(INNER, nodes, width)

    reduce_count = iter(range(n_rows))

    def give(src, dst, recv, row_to):
        post(src, dst, rs_send.at[next(reduce_count)], recv, row_to, rep)

    def taken(dst, recv):
        remote(dst, dst, rs_send.at[0], recv, at(outer, inner_x), rep).wait_recv()

    def far_terms(o):
        terms[pl.ds(pl.multiple_of(o * INNER, INNER), INNER)] = plane_product(o).astype(BF16)
        for i in plane_inners:
            give(terms.at[at(o, i)], in_far.at[o, inner], in_far_recv.at[o, inner], at(outer, i))

    def partner_terms():
        terms[pl.ds(pl.multiple_of(partner * INNER, INNER), INNER)] = plane_product(partner).astype(BF16)
        for i in plane_inners + (inner,):
            give(terms.at[at(partner, i)], in_part.at[i], in_part_recv.at[i], at(partner, inner))

    def plane_sum(i):
        taken(in_part.at[i], in_part_recv.at[i])
        c = at(outer, i)
        terms[c] = (own_plane[i] + in_part[i].astype(F32)).astype(BF16)
        give(terms.at[c], in_own.at[inner], in_own_recv.at[inner], c)

    def far_sum(o):
        c = at(o, inner)
        total = terms[c].astype(F32)
        for i in plane_inners:
            taken(in_far.at[o, i], in_far_recv.at[o, i])
            total = total + in_far[o, i].astype(F32)
        terms[c] = total.astype(BF16)
        give(terms.at[c], in_z.at[outer], in_z_recv.at[outer], c)

    w_send_terms()
    for n, o in enumerate(far_reduce):
        far_terms(o)
        if n == 0:
            partner_terms()
    if not far_reduce:
        partner_terms()
    own_plane[...] = plane_product(outer)
    plane_sum(inner_d)
    w_send_sums()
    for n, o in enumerate(far_reduce):
        far_sum(o)
        if n == 0:
            plane_sum(inner_x)
            plane_sum(inner_y)
    drain()
    taken(in_part.at[inner], in_part_recv.at[inner])
    total = own_plane[inner] + in_part[inner].astype(F32)
    w_swap()
    for i in plane_inners:
        taken(in_own.at[i], in_own_recv.at[i])
        total = total + in_own[i].astype(F32)
    w_finish()
    for o in far_reduce:
        taken(in_z.at[o], in_z_recv.at[o])
        total = total + in_z[o].astype(F32)
    fgrad_ref[...] = total.astype(BF16)
    drain()


def result_kernel(act_in, fgrad_in, wstep_0, wstep_1, wstep_2, wstep_3, act_hbm, fgrad_hbm, wstep_hbm, sems):
    rows = wstep_0.shape[0]
    pairs = [(act_in, act_hbm), (fgrad_in, fgrad_hbm)]
    pairs += [
        (part, wstep_hbm.at[pl.ds(n * rows, rows)]) for n, part in enumerate((wstep_0, wstep_1, wstep_2, wstep_3))
    ]
    copies = [pltpu.make_async_copy(src, dst, sems.at[n]) for n, (src, dst) in enumerate(pairs)]
    for copy in copies:
        copy.start()
    for copy in copies:
        copy.wait()


def body(n_rows, n_rep, features, weight, adj_tiles, tile_cols, tile_counts, out_grad, train_mask):
    nodes, width = features.shape
    tile_rows, tile = adj_tiles.shape[0], adj_tiles.shape[-1]
    outer_count = n_rows // INNER
    piece = width // n_rows
    half = width // 2
    w_type = BF16 if piece % 16 == 0 else F32
    vmem = pl.BlockSpec(memory_space=pltpu.VMEM)
    hbm = pl.BlockSpec(memory_space=pltpu.HBM)
    dma = pltpu.SemaphoreType.DMA
    vmem_bytes = int((53.5 if n_rows <= 16 else 63) * 1024 * 1024)
    block = (nodes, width)
    outs = (
        jax.ShapeDtypeStruct(block, BF16),
        jax.ShapeDtypeStruct(block, BF16),
        jax.ShapeDtypeStruct((width, width), F32),
    )
    counts = tile_counts.reshape(-1)
    results = pl.pallas_call(
        functools.partial(layer_kernel, n_rows, n_rep),
        out_shape=outs[:2] + (jax.ShapeDtypeStruct((width // PARTS, width), F32),) * PARTS,
        in_specs=[hbm] * 7,
        out_specs=(vmem,) * (2 + PARTS),
        scratch_shapes=[
            pltpu.SMEM(tile_cols.shape, jnp.int32),
            pltpu.SMEM(counts.shape, jnp.int32),
            pltpu.VMEM(weight.shape, BF16),
            pltpu.VMEM(adj_tiles.shape, BF16),
            pltpu.VMEM(block, BF16),
            pltpu.VMEM((1, nodes), jnp.int32),
            pltpu.VMEM((n_rows,) + block, BF16),
            pltpu.VMEM((tile_rows * tile, n_rows * tile), BF16),
            pltpu.VMEM((n_rows * tile, tile_rows * tile), BF16),
            pltpu.VMEM((n_rep,) + block, BF16),
            pltpu.VMEM((n_rep * nodes, width), F32),
            pltpu.VMEM((n_rep,) + block, F32),
            pltpu.VMEM((2, n_rep) + block, BF16),
            pltpu.VMEM((width, width), F32),
            pltpu.VMEM((n_rows, piece, half), w_type),
            pltpu.VMEM((n_rows, piece, half), w_type),
            pltpu.VMEM((2, n_rows, piece, half), w_type),
            pltpu.VMEM((n_rows,) + block, BF16),
            pltpu.VMEM((INNER,) + block, F32),
            pltpu.VMEM((INNER,) + block, BF16),
            pltpu.VMEM((outer_count, INNER) + block, BF16),
            pltpu.VMEM((INNER,) + block, BF16),
            pltpu.VMEM((outer_count,) + block, BF16),
            dma((7,)),
            dma((n_rows,)), dma((n_rows,)),
            dma, dma,
            dma((n_rep,)), dma((n_rep,)),
            dma((2, n_rep)), dma((2, n_rep)),
            dma((n_rows,)), dma((n_rows,)),
            dma((n_rows,)), dma((n_rows,)),
            dma, dma,
            dma((n_rows,)), dma((INNER,)), dma((outer_count, INNER)), dma((INNER,)), dma((outer_count,)),
        ],
        compiler_params=pltpu.CompilerParams(
            collective_id=0, has_side_effects=True, vmem_limit_bytes=vmem_bytes
        ),
    )(
        features, weight, adj_tiles, tile_cols, counts, out_grad, train_mask.reshape(1, -1),
    )
    return pl.pallas_call(
        result_kernel,
        out_shape=outs,
        in_specs=[pl.BlockSpec(memory_space=pl.ANY)] * (2 + PARTS),
        out_specs=(hbm, hbm, hbm),
        scratch_shapes=[dma((2 + PARTS,))],
        compiler_params=pltpu.CompilerParams(vmem_limit_bytes=256 * 1024),
    )(*results)


def solution(mesh):
    placed = (
        P(("rows", "rep"), None),
        P(),
        P("rows", "rep", None, None, None),
        P("rows", "rep", None),
        P("rows", "rep"),
        P(("rows", "rep"), None),
        P(("rows", "rep")),
    )
    return jax.shard_map(
        functools.partial(body, mesh.shape["rows"], mesh.shape["rep"]),
        mesh=mesh,
        in_specs=placed,
        out_specs=(P(("rows", "rep"), None), P(("rows", "rep"), None), P()),
        check_vma=False,
    )
```

```python
import functools

import jax
import jax.numpy as jnp
from jax import lax
from jax.experimental import pallas as pl
from jax.experimental.pallas import tpu as pltpu
from jax.sharding import PartitionSpec as P

MESH = pl.DeviceIdType.MESH
F32 = jnp.float32
BF16 = jnp.bfloat16
INNER = 4
PARTS = 4


def layer_kernel(
    n_rows, n_rep,
    feat_hbm, weight_hbm, adj_hbm, cols_hbm, counts_hbm, grad_hbm, mask_hbm,
    act_ref, fgrad_ref, wstep_0, wstep_1, wstep_2, wstep_3,
    cols_ref, counts_ref, weight_ref, adj_ref, grad_ref, mask_ref,
    panel, dense, dense_t, masked, acc, part_in, shared,
    w_full, w_out, w_in, w_all, terms, own_plane, in_part, in_far, in_own, in_z,
    load_sem, ag_send, own_recv, far_recv, plane_recv, partner_recv, masked_send, masked_recv,
    part_send, part_recv, grads_send, grads_recv, w_send, w_recv, wa_send, wa_recv, swap_send, swap_recv,
    rs_send, in_part_recv, in_far_recv, in_own_recv, in_z_recv,
):
    nodes, width = feat_hbm.shape
    tile_rows, slots, tile = adj_ref.shape[0], adj_ref.shape[2], adj_ref.shape[3]
    piece = w_out.shape[1]
    half = w_out.shape[2]
    outer_count = n_rows // INNER
    both = n_rep == 2
    block_rows = n_rep * nodes
    quarters = (wstep_0, wstep_1, wstep_2, wstep_3)
    plane_nodes = INNER * nodes
    row = lax.axis_index("rows")
    rep = lax.axis_index("rep")
    outer, inner = row // INNER, row % INNER
    iy, ix = inner // 2, inner % 2
    inner_x, inner_y = iy * 2 + (1 - ix), (1 - iy) * 2 + ix
    inner_d = (1 - iy) * 2 + (1 - ix)
    side_of = outer % 2
    partner = outer + 1 - 2 * side_of
    pair, pairs = outer // 2, outer_count // 2
    others = [(pair + d) % pairs for d in range(1, pairs)]
    far_gather = [2 * q + m for q in others for m in (1 - side_of, side_of)]
    far_reduce = [2 * q + m for q in others[::-1] for m in (side_of, 1 - side_of)]
    rep_peers = [(rep + d) % n_rep for d in range(1, n_rep)]
    row_peers = [(row + d) % n_rows for d in range(1, n_rows)]
    plane_inners = (inner_d, inner_x, inner_y)
    pending = []

    def remote(src, dst, send, recv, row_to, rep_to):
        return pltpu.make_async_remote_copy(
            src_ref=src, dst_ref=dst, send_sem=send, recv_sem=recv,
            device_id=(row_to, rep_to), device_id_type=MESH,
        )

    def post(*spec):
        copy = remote(*spec)
        copy.start()
        pending.append(copy)

    def drain():
        while pending:
            pending.pop(0).wait_send()

    def at(o, i):
        return o * INNER + i

    def other_slot(o, seen_from):
        return ((o // 2 - seen_from // 2 + pairs) % pairs - 1) * 2 + o % 2

    def plane_of(o, count=INNER):
        return pl.ds(pl.multiple_of(o * INNER, INNER), count)

    barrier = pltpu.get_barrier_semaphore()
    near = [(at(o, inner), rep) for o in [partner] + far_gather]
    near += [(at(outer, i), rep) for i in plane_inners]
    near += [(row, p) for p in rep_peers]
    for other in near:
        pl.semaphore_signal(barrier, inc=1, device_id=other, device_id_type=MESH)
    loads = [
        pltpu.make_async_copy(src, dst, load_sem.at[n])
        for n, (src, dst) in enumerate([
            (adj_hbm, adj_ref), (cols_hbm, cols_ref), (counts_hbm, counts_ref),
            (grad_hbm, grad_ref), (mask_hbm, mask_ref), (feat_hbm, panel.at[row]),
            (weight_hbm, weight_ref),
        ])
    ]
    for load in loads:
        load.start()
    pl.semaphore_wait(barrier, len(near))

    def gather(src, source, row_to, recv):
        remote(src, panel.at[source], ag_send, recv, row_to, rep).start()

    def gathered(blocks, recv):
        remote(panel.at[blocks], panel.at[blocks], ag_send, recv, at(outer, inner_x), rep).wait_recv()

    for o in far_gather:
        gather(feat_hbm, row, at(o, inner), far_recv.at[other_slot(outer, o)])
    for n, i in enumerate(plane_inners):
        gather(feat_hbm, row, at(outer, i), own_recv.at[n])
    gather(feat_hbm, row, at(partner, inner), partner_recv)
    for load in loads[:5]:
        load.wait()

    def build(r, start, stop):
        def column(c, carry):
            total = jnp.zeros((tile, tile), F32)
            for k in range(slots):
                chosen = jnp.logical_and(cols_ref[r, 0, k] == c, k < counts_ref[r])
                total = total + jnp.where(chosen, 1.0, 0.0) * adj_ref[r, 0, k].astype(F32)
            place = pl.multiple_of(c * tile, tile)
            dense[r * tile:(r + 1) * tile, pl.ds(place, tile)] = total.astype(BF16)
            dense_t[pl.ds(place, tile), r * tile:(r + 1) * tile] = total.T.astype(BF16)
            return carry

        lax.fori_loop(start, stop, column, 0)

    stride = n_rows // 8
    jobs = [(r, c, c + stride) for r in range(tile_rows) for c in range(0, n_rows, stride)]

    def build_jobs(count):
        for _ in range(min(count, len(jobs))):
            build(*jobs.pop(0))

    mask_col = jnp.broadcast_to(mask_ref[...].astype(F32), (nodes, nodes)).T
    mask = jnp.concatenate([mask_col] * (width // nodes), axis=1)
    masked[rep] = (grad_ref[...].astype(F32) * mask).astype(BF16)
    if both:
        for p in rep_peers:
            post(masked.at[rep], masked.at[rep], masked_send, masked_recv, row, p)

    def to_partner(n):
        source = at(outer, plane_inners[n])
        gathered(source, own_recv.at[n])
        gather(panel.at[source], source, at(partner, inner), partner_recv)

    def to_plane(o):
        source, slot = at(o, inner), other_slot(o, outer)
        gathered(source, far_recv.at[slot])
        for i in plane_inners:
            gather(panel.at[source], source, at(outer, i), plane_recv.at[slot])

    share = len(jobs)
    build_jobs(share * 3 // 8)
    to_partner(1)
    to_partner(2)
    for n, o in enumerate(far_gather):
        build_jobs(max(1, share // (4 * len(far_gather))) if n == 0 else max(1, share // (2 * len(far_gather))))
        to_plane(o)
        if n == 0:
            to_partner(0)
    build_jobs(len(jobs))
    for load in loads[5:]:
        load.wait()

    def product(o, rows_at):
        place = pl.multiple_of(o * plane_nodes, plane_nodes)
        planes = panel[plane_of(o)].reshape(plane_nodes, width)
        return jnp.dot(dense[rows_at, pl.ds(place, plane_nodes)], planes, preferred_element_type=F32)

    everything = pl.ds(0, block_rows)
    order = [outer] + far_gather[:-1] + [partner] + far_gather[-1:]
    for n, o in enumerate(order[:-1]):
        if n == len(order) - 2 or not far_gather:
            gathered(plane_of(partner), partner_recv)
        elif n > 0:
            gathered(plane_of(o, INNER - 1), plane_recv.at[other_slot(o, outer)])
        value = product(o, everything)
        acc[...] = value if n == 0 else acc[...] + value
    last = order[-1]
    if far_gather:
        gathered(plane_of(last, INNER - 1), plane_recv.at[other_slot(last, outer)])

    def rows_of(p):
        return pl.ds(p * nodes if isinstance(p, int) else pl.multiple_of(p * nodes, nodes), nodes)

    def finish_product(p):
        acc[rows_of(p), :] = acc[rows_of(p), :] + product(last, rows_of(p))

    def slope_of(pre_act, sigmoid):
        return sigmoid * (1.0 + pre_act * (1.0 - sigmoid))

    if both:
        other = rep_peers[0]
        for r in range(n_rep):
            finish_product(r)
            post(acc.at[rows_of(r)], part_in.at[r], part_send.at[r], part_recv.at[r], row, other)
        remote(masked.at[rep], masked.at[other], masked_send, masked_recv, row, other).wait_recv()
        for r in range(n_rep):
            remote(acc.at[rows_of(r)], part_in.at[r], part_send.at[r], part_recv.at[r], row, other).wait_recv()
            aggregated = (acc[rows_of(r), :] + part_in[r]).astype(BF16)
            shared[0, r] = aggregated
            pre_act = jnp.dot(aggregated, weight_ref[...], preferred_element_type=F32)
            sigmoid = jax.nn.sigmoid(pre_act)
            shared[1, r] = (masked[r].astype(F32) * slope_of(pre_act, sigmoid)).astype(BF16)

            @pl.when(rep == r)
            def _():
                act_ref[...] = (pre_act * sigmoid).astype(BF16)
    else:
        for d, p in enumerate(rep_peers):
            finish_product(p)
            post(acc.at[rows_of(p)], part_in.at[rep], part_send.at[d], part_recv.at[rep], row, p)
        finish_product(rep)
        total = acc[rows_of(rep), :]
        for p in rep_peers:
            remote(acc.at[rows_of(p)], part_in.at[p], part_send.at[0], part_recv.at[p], row, p).wait_recv()
            total = total + part_in[p]
        aggregated = total.astype(BF16)
        shared[0, rep] = aggregated
        for d, p in enumerate(rep_peers):
            post(shared.at[0, rep], shared.at[0, rep], grads_send.at[0, d], grads_recv.at[0, rep], row, p)
        pre_act = jnp.dot(aggregated, weight_ref[...], preferred_element_type=F32)
        sigmoid = jax.nn.sigmoid(pre_act)
        shared[1, rep] = (masked[rep].astype(F32) * slope_of(pre_act, sigmoid)).astype(BF16)
        for d, p in enumerate(rep_peers):
            post(shared.at[1, rep], shared.at[1, rep], grads_send.at[1, d], grads_recv.at[1, rep], row, p)
        act_ref[...] = (pre_act * sigmoid).astype(BF16)
        for n in range(2):
            for p in rep_peers:
                remote(shared.at[n, p], shared.at[n, p], grads_send.at[0, 0], grads_recv.at[n, p], row, p).wait_recv()

    row_pre_grads = shared[1].reshape(block_rows, width)
    row_grads = lax.dot_general(
        row_pre_grads, weight_ref[...], (((1,), (1,)), ((), ())), preferred_element_type=F32
    ).astype(BF16)

    def w_send_terms():
        column = pl.multiple_of((rep % 2) * half, half)
        w_full[...] = lax.dot_general(
            shared[0].reshape(block_rows, width), row_pre_grads,
            (((0,), (0,)), ((), ())), preferred_element_type=F32,
        )
        w_half = w_full[:, pl.ds(column, half)]
        for b in range(n_rows):
            w_out[b] = w_half[b * piece:(b + 1) * piece].astype(w_out.dtype)
        for to in row_peers:
            remote(w_out.at[to], w_in.at[row], w_send, w_recv, to, rep).start()
        w_in[row] = w_out[row]

    def w_send_sums():
        arrived = w_in.at[pl.ds(0, n_rows - 1)]
        remote(arrived, arrived, w_send, w_recv, row_peers[0], rep).wait_recv()
        side = rep % 2
        w_all[side, row] = jnp.sum(w_in[...].astype(F32), axis=0).astype(w_all.dtype)
        for to in row_peers:
            remote(w_all.at[side, row], w_all.at[side, row], wa_send, wa_recv, to, rep).start()

    def w_swap():
        side = rep % 2
        arrived = w_all.at[side, pl.ds(0, n_rows - 1)]
        remote(arrived, arrived, wa_send, wa_recv, row_peers[0], rep).wait_recv()
        post(w_all.at[side], w_all.at[side], swap_send, swap_recv, row, (rep + 1) % n_rep)

    def w_finish():
        other_side = w_all.at[(rep + 1) % 2]
        remote(other_side, other_side, swap_send, swap_recv, row, (rep + 1) % n_rep).wait_recv()
        whole = w_all[...].astype(F32)
        scale = lax.rsqrt(jnp.sum(whole * whole) / (width * width) + 1e-06)
        for side in range(2):
            for b in range(n_rows):
                ref, first = quarters[b * piece * PARTS // width], b * piece % (width // PARTS)
                ref[first:first + piece, side * half:(side + 1) * half] = whole[side, b] * scale

    def plane_product(o):
        place = pl.multiple_of(o * plane_nodes, plane_nodes)
        value = jnp.dot(dense_t[pl.ds(place, plane_nodes), :], row_grads, preferred_element_type=F32)
        return value.reshape(INNER, nodes, width)

    def give(src, dst, recv, row_to):
        remote(src, dst, rs_send, recv, row_to, rep).start()

    def taken(dst, recv):
        remote(dst, dst, rs_send, recv, at(outer, inner_x), rep).wait_recv()

    def far_terms(o):
        terms[plane_of(o)] = plane_product(o).astype(BF16)
        slot = other_slot(o, outer)
        for n, i in enumerate(plane_inners):
            give(terms.at[at(o, i)], in_far.at[slot, n], in_far_recv.at[slot], at(outer, i))

    def partner_terms():
        terms[plane_of(partner)] = plane_product(partner).astype(BF16)
        for n, i in enumerate(plane_inners + (inner,)):
            give(terms.at[at(partner, i)], in_part.at[n], in_part_recv.at[n], at(partner, inner))

    def plane_sum(n):
        taken(in_part.at[n], in_part_recv.at[n])
        i = plane_inners[n]
        c = at(outer, i)
        terms[c] = (own_plane[i] + in_part[n].astype(F32)).astype(BF16)
        give(terms.at[c], in_own.at[n], in_own_recv, c)

    def far_sum(o):
        c, slot = at(o, inner), other_slot(o, outer)
        taken(in_far.at[slot], in_far_recv.at[slot])
        total = terms[c].astype(F32)
        for n in range(INNER - 1):
            total = total + in_far[slot, n].astype(F32)
        terms[c] = total.astype(BF16)
        give(terms.at[c], in_z.at[other_slot(outer, o)], in_z_recv, c)

    w_send_terms()
    for n, o in enumerate(far_reduce):
        far_terms(o)
        if n == 0:
            partner_terms()
    if not far_reduce:
        partner_terms()
    own_plane[...] = plane_product(outer)
    plane_sum(0)
    w_send_sums()
    for n, o in enumerate(far_reduce):
        far_sum(o)
        if n == 0:
            plane_sum(1)
            plane_sum(2)
    drain()
    sent = panel.at[pl.ds(0, n_rows - 1)]
    remote(sent, sent, ag_send, partner_recv, row_peers[0], rep).wait_send()
    taken(in_part.at[INNER - 1], in_part_recv.at[INNER - 1])
    total = own_plane[inner] + in_part[INNER - 1].astype(F32)
    w_swap()
    taken(in_own, in_own_recv)
    for n in range(INNER - 1):
        total = total + in_own[n].astype(F32)
    w_finish()
    if far_reduce:
        taken(in_z, in_z_recv)
        for n in range(outer_count - 2):
            total = total + in_z[n].astype(F32)
    fgrad_ref[...] = total.astype(BF16)
    for source, send in (
        (terms.at[pl.ds(0, n_rows - 1)], rs_send), (w_out.at[pl.ds(0, n_rows - 1)], w_send),
        (w_all.at[0, pl.ds(0, n_rows - 1)], wa_send),
    ):
        remote(source, source, send, partner_recv, row_peers[0], rep).wait_send()
    drain()


def result_kernel(act_in, fgrad_in, wstep_0, wstep_1, wstep_2, wstep_3, act_hbm, fgrad_hbm, wstep_hbm, sems):
    rows = wstep_0.shape[0]
    pairs = [(act_in, act_hbm), (fgrad_in, fgrad_hbm)]
    pairs += [
        (part, wstep_hbm.at[pl.ds(n * rows, rows)]) for n, part in enumerate((wstep_0, wstep_1, wstep_2, wstep_3))
    ]
    copies = [pltpu.make_async_copy(src, dst, sems.at[n]) for n, (src, dst) in enumerate(pairs)]
    for copy in copies:
        copy.start()
    for copy in copies:
        copy.wait()


def body(n_rows, n_rep, features, weight, adj_tiles, tile_cols, tile_counts, out_grad, train_mask):
    nodes, width = features.shape
    tile_rows, tile = adj_tiles.shape[0], adj_tiles.shape[-1]
    others = max(n_rows // INNER - 2, 1)
    grads = (2, n_rep) if n_rep != 2 else (1, 1)
    piece = width // n_rows
    half = width // 2
    w_type = BF16 if piece % 16 == 0 else F32
    vmem = pl.BlockSpec(memory_space=pltpu.VMEM)
    hbm = pl.BlockSpec(memory_space=pltpu.HBM)
    dma = pltpu.SemaphoreType.DMA
    vmem_bytes = int((53.5 if n_rows <= 16 else 63) * 1024 * 1024)
    block = (nodes, width)
    outs = (
        jax.ShapeDtypeStruct(block, BF16),
        jax.ShapeDtypeStruct(block, BF16),
        jax.ShapeDtypeStruct((width, width), F32),
    )
    counts = tile_counts.reshape(-1)
    results = pl.pallas_call(
        functools.partial(layer_kernel, n_rows, n_rep),
        out_shape=outs[:2] + (jax.ShapeDtypeStruct((width // PARTS, width), F32),) * PARTS,
        in_specs=[hbm] * 7,
        out_specs=(vmem,) * (2 + PARTS),
        scratch_shapes=[
            pltpu.SMEM(tile_cols.shape, jnp.int32),
            pltpu.SMEM(counts.shape, jnp.int32),
            pltpu.VMEM(weight.shape, BF16),
            pltpu.VMEM(adj_tiles.shape, BF16),
            pltpu.VMEM(block, BF16),
            pltpu.VMEM((1, nodes), jnp.int32),
            pltpu.VMEM((n_rows,) + block, BF16),
            pltpu.VMEM((tile_rows * tile, n_rows * tile), BF16),
            pltpu.VMEM((n_rows * tile, tile_rows * tile), BF16),
            pltpu.VMEM((n_rep,) + block, BF16),
            pltpu.VMEM((n_rep * nodes, width), F32),
            pltpu.VMEM((n_rep,) + block, F32),
            pltpu.VMEM((2, n_rep) + block, BF16),
            pltpu.VMEM((width, width), F32),
            pltpu.VMEM((n_rows, piece, half), w_type),
            pltpu.VMEM((n_rows, piece, half), w_type),
            pltpu.VMEM((2, n_rows, piece, half), w_type),
            pltpu.VMEM((n_rows,) + block, BF16),
            pltpu.VMEM((INNER,) + block, F32),
            pltpu.VMEM((INNER,) + block, BF16),
            pltpu.VMEM((others, INNER - 1) + block, BF16),
            pltpu.VMEM((INNER - 1,) + block, BF16),
            pltpu.VMEM((others,) + block, BF16),
            dma((7,)),
            dma, dma((INNER - 1,)), dma((others,)), dma((others,)), dma,
            dma, dma,
            dma((n_rep,)), dma((n_rep,)),
            dma(grads), dma(grads),
            dma, dma, dma, dma,
            dma, dma,
            dma, dma((INNER,)), dma((others,)), dma, dma,
        ],
        compiler_params=pltpu.CompilerParams(
            collective_id=0, has_side_effects=True, vmem_limit_bytes=vmem_bytes
        ),
    )(
        features, weight, adj_tiles, tile_cols, counts, out_grad, train_mask.reshape(1, -1),
    )
    return pl.pallas_call(
        result_kernel,
        out_shape=outs,
        in_specs=[pl.BlockSpec(memory_space=pl.ANY)] * (2 + PARTS),
        out_specs=(hbm, hbm, hbm),
        scratch_shapes=[dma((2 + PARTS,))],
        compiler_params=pltpu.CompilerParams(vmem_limit_bytes=256 * 1024),
    )(*results)


def solution(mesh):
    placed = (
        P(("rows", "rep"), None),
        P(),
        P("rows", "rep", None, None, None),
        P("rows", "rep", None),
        P("rows", "rep"),
        P(("rows", "rep"), None),
        P(("rows", "rep")),
    )
    return jax.shard_map(
        functools.partial(body, mesh.shape["rows"], mesh.shape["rep"]),
        mesh=mesh,
        in_specs=placed,
        out_specs=(P(("rows", "rep"), None), P(("rows", "rep"), None), P()),
        check_vma=False,
    )
```

```python
import functools

import jax
import jax.numpy as jnp
from jax import lax
from jax.experimental import pallas as pl
from jax.experimental.pallas import tpu as pltpu
from jax.sharding import PartitionSpec as P

MESH = pl.DeviceIdType.MESH
F32 = jnp.float32
BF16 = jnp.bfloat16
INNER = 4


def layer_kernel(
    n_rows, n_rep,
    feat_hbm, weight_hbm, adj_hbm, cols_hbm, counts_hbm, grad_hbm, mask_hbm,
    act_ref, fgrad_ref, wstep_ref,
    cols_ref, counts_ref, weight_ref, adj_ref, grad_ref, mask_ref,
    panel, dense, dense_t, masked, acc, part_in, shared,
    w_full, w_out, w_in, w_all, terms, own_plane, in_part, in_far, in_own, in_z,
    load_sem, ag_send, own_recv, far_recv, plane_recv, partner_recv, masked_send, masked_recv,
    part_send, part_recv, grads_send, grads_recv, w_send, w_recv, wa_send, wa_recv, swap_send, swap_recv,
    rs_send, in_part_recv, in_far_recv, in_own_recv, in_z_recv,
):
    nodes, width = feat_hbm.shape
    tile_rows, slots, tile = adj_ref.shape[0], adj_ref.shape[2], adj_ref.shape[3]
    piece = w_out.shape[1]
    half = w_out.shape[2]
    outer_count = n_rows // INNER
    both = n_rep == 2
    block_rows = n_rep * nodes
    plane_nodes = INNER * nodes
    row = lax.axis_index("rows")
    rep = lax.axis_index("rep")
    outer, inner = row // INNER, row % INNER
    iy, ix = inner // 2, inner % 2
    inner_x, inner_y = iy * 2 + (1 - ix), (1 - iy) * 2 + ix
    inner_d = (1 - iy) * 2 + (1 - ix)
    side_of = outer % 2
    partner = outer + 1 - 2 * side_of
    pair, pairs = outer // 2, outer_count // 2
    others = [(pair + d) % pairs for d in range(1, pairs)]
    far_gather = [2 * q + m for q in others for m in (1 - side_of, side_of)]
    far_reduce = [2 * q + m for q in others[::-1] for m in (side_of, 1 - side_of)]
    rep_peers = [(rep + d) % n_rep for d in range(1, n_rep)]
    row_peers = [(row + d) % n_rows for d in range(1, n_rows)]
    plane_inners = (inner_d, inner_x, inner_y)
    halves = [pl.ds(h * (nodes // 2), nodes // 2) for h in range(2)]
    pending = []

    def remote(src, dst, send, recv, row_to, rep_to):
        return pltpu.make_async_remote_copy(
            src_ref=src, dst_ref=dst, send_sem=send, recv_sem=recv,
            device_id=(row_to, rep_to), device_id_type=MESH,
        )

    def post(*spec):
        copy = remote(*spec)
        copy.start()
        pending.append(copy)

    def drain():
        while pending:
            pending.pop(0).wait_send()

    def at(o, i):
        return o * INNER + i

    def other_slot(o, seen_from):
        return ((o // 2 - seen_from // 2 + pairs) % pairs - 1) * 2 + o % 2

    def plane_of(o, count=INNER):
        return pl.ds(pl.multiple_of(o * INNER, INNER), count)

    barrier = pltpu.get_barrier_semaphore()
    near = [(at(o, inner), rep) for o in [partner] + far_gather]
    near += [(at(outer, i), rep) for i in plane_inners]
    near += [(row, p) for p in rep_peers]
    for other in near:
        pl.semaphore_signal(barrier, inc=1, device_id=other, device_id_type=MESH)
    loads = [
        pltpu.make_async_copy(src, dst, load_sem.at[n])
        for n, (src, dst) in enumerate([
            (adj_hbm, adj_ref), (cols_hbm, cols_ref), (counts_hbm, counts_ref),
            (grad_hbm, grad_ref), (mask_hbm, mask_ref), (feat_hbm, panel.at[row]),
            (weight_hbm, weight_ref),
        ])
    ]
    for load in loads:
        load.start()
    pl.semaphore_wait(barrier, len(near))

    def gather(src, source, row_to, recv):
        for h in range(2):
            remote(src.at[halves[h]], panel.at[source, halves[h]], ag_send, recv[h], row_to, rep).start()

    def gathered(blocks, recv):
        remote(panel.at[blocks], panel.at[blocks], ag_send, recv, at(outer, inner_x), rep).wait_recv()

    for o in far_gather:
        gather(feat_hbm, row, at(o, inner), [far_recv.at[other_slot(outer, o), h] for h in range(2)])
    for n, i in enumerate(plane_inners):
        gather(feat_hbm, row, at(outer, i), [own_recv.at[n, h] for h in range(2)])
    gather(feat_hbm, row, at(partner, inner), [partner_recv] * 2)
    for load in loads[:5]:
        load.wait()

    def build(r, start, stop):
        def column(c, carry):
            total = jnp.zeros((tile, tile), F32)
            for k in range(slots):
                chosen = jnp.logical_and(cols_ref[r, 0, k] == c, k < counts_ref[r])
                total = total + jnp.where(chosen, 1.0, 0.0) * adj_ref[r, 0, k].astype(F32)
            place = pl.multiple_of(c * tile, tile)
            dense[r * tile:(r + 1) * tile, pl.ds(place, tile)] = total.astype(BF16)
            dense_t[pl.ds(place, tile), r * tile:(r + 1) * tile] = total.T.astype(BF16)
            return carry

        lax.fori_loop(start, stop, column, 0)

    stride = n_rows // 8
    jobs = [(r, c, c + stride) for r in range(tile_rows) for c in range(0, n_rows, stride)]

    def build_jobs(count):
        for _ in range(min(count, len(jobs))):
            build(*jobs.pop(0))

    mask_col = jnp.broadcast_to(mask_ref[...].astype(F32), (nodes, nodes)).T
    mask = jnp.concatenate([mask_col] * (width // nodes), axis=1)
    masked[rep] = (grad_ref[...].astype(F32) * mask).astype(BF16)
    if both:
        for p in rep_peers:
            post(masked.at[rep], masked.at[rep], masked_send, masked_recv, row, p)

    def pass_on(source, recvs, targets, recv):
        for h in range(2):
            half_block = panel.at[source, halves[h]]
            remote(half_block, half_block, ag_send, recvs.at[h], at(outer, inner_x), rep).wait_recv()
            for to in targets:
                remote(half_block, half_block, ag_send, recv, to, rep).start()

    def to_partner(n):
        pass_on(at(outer, plane_inners[n]), own_recv.at[n], [at(partner, inner)], partner_recv)

    def to_plane(o):
        slot = other_slot(o, outer)
        pass_on(at(o, inner), far_recv.at[slot], [at(outer, i) for i in plane_inners], plane_recv.at[slot])

    share = len(jobs)
    build_jobs(share * 3 // 8)
    to_partner(1)
    to_partner(2)
    for n, o in enumerate(far_gather):
        build_jobs(max(1, share // (4 * len(far_gather))) if n == 0 else max(1, share // (2 * len(far_gather))))
        to_plane(o)
        if n == 0:
            to_partner(0)
    build_jobs(len(jobs))
    for load in loads[5:]:
        load.wait()

    def product(o, rows_at):
        place = pl.multiple_of(o * plane_nodes, plane_nodes)
        planes = panel[plane_of(o)].reshape(plane_nodes, width)
        return jnp.dot(dense[rows_at, pl.ds(place, plane_nodes)], planes, preferred_element_type=F32)

    everything = pl.ds(0, block_rows)
    order = [outer] + far_gather[:-1] + [partner] + far_gather[-1:]
    for n, o in enumerate(order[:-1]):
        if n == len(order) - 2 or not far_gather:
            gathered(plane_of(partner), partner_recv)
        elif n > 0:
            gathered(plane_of(o, INNER - 1), plane_recv.at[other_slot(o, outer)])
        value = product(o, everything)
        acc[...] = value if n == 0 else acc[...] + value
    last = order[-1]
    if far_gather:
        gathered(plane_of(last, INNER - 1), plane_recv.at[other_slot(last, outer)])

    def rows_of(p):
        return pl.ds(p * nodes if isinstance(p, int) else pl.multiple_of(p * nodes, nodes), nodes)

    def finish_product(p):
        acc[rows_of(p), :] = acc[rows_of(p), :] + product(last, rows_of(p))

    def slope_of(pre_act, sigmoid):
        return sigmoid * (1.0 + pre_act * (1.0 - sigmoid))

    if both:
        other = rep_peers[0]
        for r in range(n_rep):
            finish_product(r)
            post(acc.at[rows_of(r)], part_in.at[r], part_send.at[r], part_recv.at[r], row, other)
        remote(masked.at[rep], masked.at[other], masked_send, masked_recv, row, other).wait_recv()
        for r in range(n_rep):
            remote(acc.at[rows_of(r)], part_in.at[r], part_send.at[r], part_recv.at[r], row, other).wait_recv()
            aggregated = (acc[rows_of(r), :] + part_in[r]).astype(BF16)
            shared[0, r] = aggregated
            pre_act = jnp.dot(aggregated, weight_ref[...], preferred_element_type=F32)
            sigmoid = jax.nn.sigmoid(pre_act)
            shared[1, r] = (masked[r].astype(F32) * slope_of(pre_act, sigmoid)).astype(BF16)

            @pl.when(rep == r)
            def _():
                act_ref[...] = (pre_act * sigmoid).astype(BF16)
    else:
        for d, p in enumerate(rep_peers):
            finish_product(p)
            post(acc.at[rows_of(p)], part_in.at[rep], part_send.at[d], part_recv.at[rep], row, p)
        finish_product(rep)
        total = acc[rows_of(rep), :]
        for p in rep_peers:
            remote(acc.at[rows_of(p)], part_in.at[p], part_send.at[0], part_recv.at[p], row, p).wait_recv()
            total = total + part_in[p]
        aggregated = total.astype(BF16)
        shared[0, rep] = aggregated
        for d, p in enumerate(rep_peers):
            post(shared.at[0, rep], shared.at[0, rep], grads_send.at[0, d], grads_recv.at[0, rep], row, p)
        pre_act = jnp.dot(aggregated, weight_ref[...], preferred_element_type=F32)
        sigmoid = jax.nn.sigmoid(pre_act)
        shared[1, rep] = (masked[rep].astype(F32) * slope_of(pre_act, sigmoid)).astype(BF16)
        for d, p in enumerate(rep_peers):
            post(shared.at[1, rep], shared.at[1, rep], grads_send.at[1, d], grads_recv.at[1, rep], row, p)
        act_ref[...] = (pre_act * sigmoid).astype(BF16)
        for n in range(2):
            for p in rep_peers:
                remote(shared.at[n, p], shared.at[n, p], grads_send.at[0, 0], grads_recv.at[n, p], row, p).wait_recv()

    row_pre_grads = shared[1].reshape(block_rows, width)
    row_grads = lax.dot_general(
        row_pre_grads, weight_ref[...], (((1,), (1,)), ((), ())), preferred_element_type=F32
    ).astype(BF16)

    def w_send_terms():
        column = pl.multiple_of((rep % 2) * half, half)
        w_full[...] = lax.dot_general(
            shared[0].reshape(block_rows, width), row_pre_grads,
            (((0,), (0,)), ((), ())), preferred_element_type=F32,
        )
        w_half = w_full[:, pl.ds(column, half)]
        for b in range(n_rows):
            w_out[b] = w_half[b * piece:(b + 1) * piece].astype(w_out.dtype)
        for to in row_peers:
            remote(w_out.at[to], w_in.at[row], w_send, w_recv, to, rep).start()
        w_in[row] = w_out[row]

    def w_send_sums():
        arrived = w_in.at[pl.ds(0, n_rows - 1)]
        remote(arrived, arrived, w_send, w_recv, row_peers[0], rep).wait_recv()
        side = rep % 2
        w_all[side, row] = jnp.sum(w_in[...].astype(F32), axis=0).astype(w_all.dtype)
        for to in row_peers:
            remote(w_all.at[side, row], w_all.at[side, row], wa_send, wa_recv, to, rep).start()

    def w_swap():
        side = rep % 2
        arrived = w_all.at[side, pl.ds(0, n_rows - 1)]
        remote(arrived, arrived, wa_send, wa_recv, row_peers[0], rep).wait_recv()
        post(w_all.at[side], w_all.at[side], swap_send, swap_recv, row, (rep + 1) % n_rep)

    def w_finish():
        other_side = w_all.at[(rep + 1) % 2]
        remote(other_side, other_side, swap_send, swap_recv, row, (rep + 1) % n_rep).wait_recv()
        whole = w_all[...].astype(F32)
        scale = lax.rsqrt(jnp.sum(whole * whole) / (width * width) + 1e-06)
        for side in range(2):
            for b in range(n_rows):
                wstep_ref[b * piece:(b + 1) * piece, side * half:(side + 1) * half] = whole[side, b] * scale

    def plane_product(o):
        place = pl.multiple_of(o * plane_nodes, plane_nodes)
        value = jnp.dot(dense_t[pl.ds(place, plane_nodes), :], row_grads, preferred_element_type=F32)
        return value.reshape(INNER, nodes, width)

    def give(src, dst, recv, row_to):
        remote(src, dst, rs_send, recv, row_to, rep).start()

    def taken(dst, recv):
        remote(dst, dst, rs_send, recv, at(outer, inner_x), rep).wait_recv()

    def far_terms(o):
        terms[plane_of(o)] = plane_product(o).astype(BF16)
        slot = other_slot(o, outer)
        for h in range(2):
            for n, i in enumerate(plane_inners):
                give(
                    terms.at[at(o, i), halves[h]], in_far.at[slot, h, n], in_far_recv.at[slot, h], at(outer, i),
                )

    def partner_terms():
        terms[plane_of(partner)] = plane_product(partner).astype(BF16)
        for n, i in enumerate(plane_inners + (inner,)):
            for h in range(2):
                give(
                    terms.at[at(partner, i), halves[h]], in_part.at[n, halves[h]],
                    in_part_recv.at[n, h], at(partner, inner),
                )

    def plane_sum(n):
        i = plane_inners[n]
        c = at(outer, i)
        for rows_at, recv in ((halves[0], in_part_recv.at[n, 0]), (halves[1], in_part_recv.at[n, 1])):
            taken(in_part.at[n, rows_at], recv)
            terms[c, rows_at] = (own_plane[i, rows_at] + in_part[n, rows_at].astype(F32)).astype(BF16)
            give(terms.at[c, rows_at], in_own.at[n, rows_at], in_own_recv, c)

    def far_sum(o):
        c, slot = at(o, inner), other_slot(o, outer)
        for h in range(2):
            taken(in_far.at[slot, h], in_far_recv.at[slot, h])
            total = terms[c, halves[h]].astype(F32)
            for n in range(INNER - 1):
                total = total + in_far[slot, h, n].astype(F32)
            terms[c, halves[h]] = total.astype(BF16)
            give(terms.at[c, halves[h]], in_z.at[other_slot(outer, o), halves[h]], in_z_recv, c)

    w_send_terms()
    for n, o in enumerate(far_reduce):
        far_terms(o)
        if n == 0:
            partner_terms()
    if not far_reduce:
        partner_terms()
    own_plane[...] = plane_product(outer)
    plane_sum(0)
    w_send_sums()
    for n, o in enumerate(far_reduce):
        far_sum(o)
        if n == 0:
            plane_sum(1)
            plane_sum(2)
    drain()
    sent = panel.at[pl.ds(0, n_rows - 1)]
    remote(sent, sent, ag_send, partner_recv, row_peers[0], rep).wait_send()
    for h in range(2):
        taken(in_part.at[INNER - 1, halves[h]], in_part_recv.at[INNER - 1, h])
    total = own_plane[inner] + in_part[INNER - 1].astype(F32)
    w_swap()
    taken(in_own, in_own_recv)
    for n in range(INNER - 1):
        total = total + in_own[n].astype(F32)
    w_finish()
    if far_reduce:
        taken(in_z, in_z_recv)
        for n in range(outer_count - 2):
            total = total + in_z[n].astype(F32)
    fgrad_ref[...] = total.astype(BF16)
    for source, send in (
        (terms.at[pl.ds(0, n_rows - 1)], rs_send), (w_out.at[pl.ds(0, n_rows - 1)], w_send),
        (w_all.at[0, pl.ds(0, n_rows - 1)], wa_send),
    ):
        remote(source, source, send, partner_recv, row_peers[0], rep).wait_send()
    drain()


def result_kernel(act_ref, fgrad_ref, wstep_ref, act_hbm, fgrad_hbm, wstep_hbm, sems):
    copies = [
        pltpu.make_async_copy(src, dst, sems.at[n])
        for n, (src, dst) in enumerate([(act_ref, act_hbm), (fgrad_ref, fgrad_hbm), (wstep_ref, wstep_hbm)])
    ]
    for copy in copies:
        copy.start()
    for copy in copies:
        copy.wait()


def body(n_rows, n_rep, features, weight, adj_tiles, tile_cols, tile_counts, out_grad, train_mask):
    nodes, width = features.shape
    tile_rows, tile = adj_tiles.shape[0], adj_tiles.shape[-1]
    others = max(n_rows // INNER - 2, 1)
    grads = (2, n_rep) if n_rep != 2 else (1, 1)
    piece = width // n_rows
    half = width // 2
    w_type = BF16 if piece % 16 == 0 else F32
    vmem = pl.BlockSpec(memory_space=pltpu.VMEM)
    hbm = pl.BlockSpec(memory_space=pltpu.HBM)
    dma = pltpu.SemaphoreType.DMA
    vmem_bytes = int((40 if n_rows <= 16 else 63) * 1024 * 1024)
    block = (nodes, width)
    outs = (
        jax.ShapeDtypeStruct(block, BF16),
        jax.ShapeDtypeStruct(block, BF16),
        jax.ShapeDtypeStruct((width, width), F32),
    )
    counts = tile_counts.reshape(-1)
    results = pl.pallas_call(
        functools.partial(layer_kernel, n_rows, n_rep),
        out_shape=tuple(pltpu.VMEM(out.shape, out.dtype) for out in outs),
        in_specs=[hbm] * 7,
        out_specs=(vmem, vmem, vmem),
        scratch_shapes=[
            pltpu.SMEM(tile_cols.shape, jnp.int32),
            pltpu.SMEM(counts.shape, jnp.int32),
            pltpu.VMEM(weight.shape, BF16),
            pltpu.VMEM(adj_tiles.shape, BF16),
            pltpu.VMEM(block, BF16),
            pltpu.VMEM((1, nodes), jnp.int32),
            pltpu.VMEM((n_rows,) + block, BF16),
            pltpu.VMEM((tile_rows * tile, n_rows * tile), BF16),
            pltpu.VMEM((n_rows * tile, tile_rows * tile), BF16),
            pltpu.VMEM((n_rep,) + block, BF16),
            pltpu.VMEM((n_rep * nodes, width), F32),
            pltpu.VMEM((n_rep,) + block, F32),
            pltpu.VMEM((2, n_rep) + block, BF16),
            pltpu.VMEM((width, width), F32),
            pltpu.VMEM((n_rows, piece, half), w_type),
            pltpu.VMEM((n_rows, piece, half), w_type),
            pltpu.VMEM((2, n_rows, piece, half), w_type),
            pltpu.VMEM((n_rows,) + block, BF16),
            pltpu.VMEM((INNER,) + block, F32),
            pltpu.VMEM((INNER,) + block, BF16),
            pltpu.VMEM((others, 2, INNER - 1, nodes // 2, width), BF16),
            pltpu.VMEM((INNER - 1,) + block, BF16),
            pltpu.VMEM((others,) + block, BF16),
            dma((7,)),
            dma, dma((INNER - 1, 2)), dma((others, 2)), dma((others,)), dma,
            dma, dma,
            dma((n_rep,)), dma((n_rep,)),
            dma(grads), dma(grads),
            dma, dma, dma, dma,
            dma, dma,
            dma, dma((INNER, 2)), dma((others, 2)), dma, dma,
        ],
        compiler_params=pltpu.CompilerParams(
            collective_id=0, has_side_effects=True, vmem_limit_bytes=vmem_bytes
        ),
    )(*[
        pltpu.with_memory_space_constraint(operand, pltpu.HBM)
        for operand in (features, weight, adj_tiles, tile_cols, counts, out_grad, train_mask.reshape(1, -1))
    ])
    return pl.pallas_call(
        result_kernel,
        out_shape=outs,
        in_specs=[vmem] * 3,
        out_specs=(hbm, hbm, hbm),
        scratch_shapes=[dma((3,))],
        compiler_params=pltpu.CompilerParams(vmem_limit_bytes=256 * 1024),
    )(*[pltpu.with_memory_space_constraint(result, pltpu.VMEM) for result in results])


def solution(mesh):
    placed = (
        P(("rows", "rep"), None),
        P(),
        P("rows", "rep", None, None, None),
        P("rows", "rep", None),
        P("rows", "rep"),
        P(("rows", "rep"), None),
        P(("rows", "rep")),
    )
    return jax.shard_map(
        functools.partial(body, mesh.shape["rows"], mesh.shape["rep"]),
        mesh=mesh,
        in_specs=placed,
        out_specs=(P(("rows", "rep"), None), P(("rows", "rep"), None), P()),
        check_vma=False,
    )
```

```python
import functools

import jax
import jax.numpy as jnp
from jax import lax
from jax.experimental import pallas as pl
from jax.experimental.pallas import tpu as pltpu
from jax.sharding import PartitionSpec as P

MESH = pl.DeviceIdType.MESH
F32 = jnp.float32
BF16 = jnp.bfloat16
INNER = 4


def layer_kernel(
    n_rows, n_rep,
    feat_hbm, weight_hbm, adj_hbm, cols_hbm, counts_hbm, grad_hbm, mask_hbm,
    act_ref, fgrad_ref, wstep_ref,
    cols_ref, counts_ref, weight_ref, adj_ref, grad_ref, mask_ref,
    panel, dense, dense_t, masked, acc, part_in, shared,
    w_full, w_out, w_in, w_all, terms, own_plane, in_part, in_far, in_own, in_z,
    load_sem, ag_send, own_recv, far_recv, plane_recv, partner_recv, masked_send, masked_recv,
    part_send, part_recv, grads_send, grads_recv, w_send, w_recv, wa_send, wa_recv, swap_send, swap_recv,
    rs_send, in_part_recv, in_far_recv, in_own_recv, in_z_recv,
):
    nodes, width = feat_hbm.shape
    tile_rows, slots, tile = adj_ref.shape[0], adj_ref.shape[2], adj_ref.shape[3]
    piece = w_out.shape[1]
    half = w_out.shape[2]
    outer_count = n_rows // INNER
    both = n_rep == 2
    block_rows = n_rep * nodes
    plane_nodes = INNER * nodes
    row = lax.axis_index("rows")
    rep = lax.axis_index("rep")
    outer, inner = row // INNER, row % INNER
    iy, ix = inner // 2, inner % 2
    inner_x, inner_y = iy * 2 + (1 - ix), (1 - iy) * 2 + ix
    inner_d = (1 - iy) * 2 + (1 - ix)
    side_of = outer % 2
    partner = outer + 1 - 2 * side_of
    pair, pairs = outer // 2, outer_count // 2
    others = [(pair + d) % pairs for d in range(1, pairs)]
    far_gather = [2 * q + m for q in others for m in (1 - side_of, side_of)]
    far_reduce = [2 * q + m for q in others[::-1] for m in (side_of, 1 - side_of)]
    rep_peers = [(rep + d) % n_rep for d in range(1, n_rep)]
    row_peers = [(row + d) % n_rows for d in range(1, n_rows)]
    plane_inners = (inner_d, inner_x, inner_y)
    halves = [pl.ds(h * (nodes // 2), nodes // 2) for h in range(2)]
    pending = []

    def remote(src, dst, send, recv, row_to, rep_to):
        return pltpu.make_async_remote_copy(
            src_ref=src, dst_ref=dst, send_sem=send, recv_sem=recv,
            device_id=(row_to, rep_to), device_id_type=MESH,
        )

    def post(*spec):
        copy = remote(*spec)
        copy.start()
        pending.append(copy)

    def drain():
        while pending:
            pending.pop(0).wait_send()

    def at(o, i):
        return o * INNER + i

    def other_slot(o, seen_from):
        return ((o // 2 - seen_from // 2 + pairs) % pairs - 1) * 2 + o % 2

    def plane_of(o, count=INNER):
        return pl.ds(pl.multiple_of(o * INNER, INNER), count)

    barrier = pltpu.get_barrier_semaphore()
    near = [(at(o, inner), rep) for o in [partner] + far_gather]
    near += [(at(outer, i), rep) for i in plane_inners]
    near += [(row, p) for p in rep_peers]
    loads = [
        pltpu.make_async_copy(src, dst, load_sem.at[n])
        for n, (src, dst) in enumerate([
            (adj_hbm, adj_ref), (cols_hbm, cols_ref), (counts_hbm, counts_ref),
            (grad_hbm, grad_ref), (mask_hbm, mask_ref), (weight_hbm, weight_ref), (feat_hbm, panel.at[row]),
        ])
    ]
    loads[-1].start()
    for other in near:
        pl.semaphore_signal(barrier, inc=1, device_id=other, device_id_type=MESH)
    for load in loads[:-1]:
        load.start()
    pl.semaphore_wait(barrier, len(near))
    loads[-1].wait()

    def gather(src, source, row_to, recv):
        for h in range(2):
            remote(src.at[halves[h]], panel.at[source, halves[h]], ag_send, recv[h], row_to, rep).start()

    def gathered(blocks, recv):
        remote(panel.at[blocks], panel.at[blocks], ag_send, recv, at(outer, inner_x), rep).wait_recv()

    for o in far_gather:
        gather(panel.at[row], row, at(o, inner), [far_recv.at[other_slot(outer, o), h] for h in range(2)])
    for n, i in enumerate(plane_inners):
        gather(panel.at[row], row, at(outer, i), [own_recv.at[n, h] for h in range(2)])
    gather(panel.at[row], row, at(partner, inner), [partner_recv] * 2)
    for load in loads[:5]:
        load.wait()

    def build(r, start, stop):
        def column(c, carry):
            total = jnp.zeros((tile, tile), F32)
            for k in range(slots):
                chosen = jnp.logical_and(cols_ref[r, 0, k] == c, k < counts_ref[r])
                total = total + jnp.where(chosen, 1.0, 0.0) * adj_ref[r, 0, k].astype(F32)
            place = pl.multiple_of(c * tile, tile)
            dense[r * tile:(r + 1) * tile, pl.ds(place, tile)] = total.astype(BF16)
            dense_t[pl.ds(place, tile), r * tile:(r + 1) * tile] = total.T.astype(BF16)
            return carry

        lax.fori_loop(start, stop, column, 0)

    stride = n_rows // 8
    jobs = [(r, c, c + stride) for r in range(tile_rows) for c in range(0, n_rows, stride)]

    def build_jobs(count):
        for _ in range(min(count, len(jobs))):
            build(*jobs.pop(0))

    mask_col = jnp.broadcast_to(mask_ref[...].astype(F32), (nodes, nodes)).T
    mask = jnp.concatenate([mask_col] * (width // nodes), axis=1)
    masked[rep] = (grad_ref[...].astype(F32) * mask).astype(BF16)
    if both:
        for p in rep_peers:
            post(masked.at[rep], masked.at[rep], masked_send, masked_recv, row, p)

    def pass_on(source, recvs, targets, recv):
        for h in range(2):
            half_block = panel.at[source, halves[h]]
            remote(half_block, half_block, ag_send, recvs.at[h], at(outer, inner_x), rep).wait_recv()
            for to in targets:
                remote(half_block, half_block, ag_send, recv, to, rep).start()

    def to_partner(n):
        pass_on(at(outer, plane_inners[n]), own_recv.at[n], [at(partner, inner)], partner_recv)

    def to_plane(o):
        slot = other_slot(o, outer)
        pass_on(at(o, inner), far_recv.at[slot], [at(outer, i) for i in plane_inners], plane_recv.at[slot])

    share = len(jobs)
    build_jobs(share // 4)
    to_partner(1)
    to_partner(2)
    for n, o in enumerate(far_gather):
        if n > 0:
            build_jobs(max(1, share // (8 * (len(far_gather) - 1))))
        to_plane(o)
        if n == 0:
            to_partner(0)
    build_jobs(len(jobs))
    loads[5].wait()

    def product(o, rows_at):
        place = pl.multiple_of(o * plane_nodes, plane_nodes)
        planes = panel[plane_of(o)].reshape(plane_nodes, width)
        return jnp.dot(dense[rows_at, pl.ds(place, plane_nodes)], planes, preferred_element_type=F32)

    everything = pl.ds(0, block_rows)
    order = [outer] + far_gather[:-1] + [partner] + far_gather[-1:]
    for n, o in enumerate(order[:-1]):
        if n == len(order) - 2 or not far_gather:
            gathered(plane_of(partner), partner_recv)
        elif n > 0:
            gathered(plane_of(o, INNER - 1), plane_recv.at[other_slot(o, outer)])
        value = product(o, everything)
        acc[...] = value if n == 0 else acc[...] + value
    last = order[-1]
    if far_gather:
        gathered(plane_of(last, INNER - 1), plane_recv.at[other_slot(last, outer)])

    def rows_of(p):
        return pl.ds(p * nodes if isinstance(p, int) else pl.multiple_of(p * nodes, nodes), nodes)

    def finish_product(p):
        acc[rows_of(p), :] = acc[rows_of(p), :] + product(last, rows_of(p))

    def slope_of(pre_act, sigmoid):
        return sigmoid * (1.0 + pre_act * (1.0 - sigmoid))

    if both:
        other = rep_peers[0]
        for r in range(n_rep):
            finish_product(r)
            post(acc.at[rows_of(r)], part_in.at[r], part_send.at[r], part_recv.at[r], row, other)
        remote(masked.at[rep], masked.at[other], masked_send, masked_recv, row, other).wait_recv()
        for r in range(n_rep):
            remote(acc.at[rows_of(r)], part_in.at[r], part_send.at[r], part_recv.at[r], row, other).wait_recv()
            aggregated = (acc[rows_of(r), :] + part_in[r]).astype(BF16)
            shared[0, r] = aggregated
            pre_act = jnp.dot(aggregated, weight_ref[...], preferred_element_type=F32)
            sigmoid = jax.nn.sigmoid(pre_act)
            shared[1, r] = (masked[r].astype(F32) * slope_of(pre_act, sigmoid)).astype(BF16)

            @pl.when(rep == r)
            def _():
                act_ref[...] = (pre_act * sigmoid).astype(BF16)
    else:
        for d, p in enumerate(rep_peers):
            finish_product(p)
            post(acc.at[rows_of(p)], part_in.at[rep], part_send.at[d], part_recv.at[rep], row, p)
        finish_product(rep)
        total = acc[rows_of(rep), :]
        for p in rep_peers:
            remote(acc.at[rows_of(p)], part_in.at[p], part_send.at[0], part_recv.at[p], row, p).wait_recv()
            total = total + part_in[p]
        aggregated = total.astype(BF16)
        shared[0, rep] = aggregated
        for d, p in enumerate(rep_peers):
            post(shared.at[0, rep], shared.at[0, rep], grads_send.at[0, d], grads_recv.at[0, rep], row, p)
        pre_act = jnp.dot(aggregated, weight_ref[...], preferred_element_type=F32)
        sigmoid = jax.nn.sigmoid(pre_act)
        shared[1, rep] = (masked[rep].astype(F32) * slope_of(pre_act, sigmoid)).astype(BF16)
        for d, p in enumerate(rep_peers):
            post(shared.at[1, rep], shared.at[1, rep], grads_send.at[1, d], grads_recv.at[1, rep], row, p)
        act_ref[...] = (pre_act * sigmoid).astype(BF16)
        for n in range(2):
            for p in rep_peers:
                remote(shared.at[n, p], shared.at[n, p], grads_send.at[0, 0], grads_recv.at[n, p], row, p).wait_recv()

    row_pre_grads = shared[1].reshape(block_rows, width)
    row_grads = lax.dot_general(
        row_pre_grads, weight_ref[...], (((1,), (1,)), ((), ())), preferred_element_type=F32
    ).astype(BF16)

    def w_send_terms():
        column = pl.multiple_of((rep % 2) * half, half)
        w_full[...] = lax.dot_general(
            shared[0].reshape(block_rows, width), row_pre_grads,
            (((0,), (0,)), ((), ())), preferred_element_type=F32,
        )
        w_half = w_full[:, pl.ds(column, half)]
        for b in range(n_rows):
            w_out[b] = w_half[b * piece:(b + 1) * piece].astype(w_out.dtype)
        for to in row_peers:
            remote(w_out.at[to], w_in.at[row], w_send, w_recv, to, rep).start()
        w_in[row] = w_out[row]

    def w_send_sums():
        arrived = w_in.at[pl.ds(0, n_rows - 1)]
        remote(arrived, arrived, w_send, w_recv, row_peers[0], rep).wait_recv()
        side = rep % 2
        w_all[side, row] = jnp.sum(w_in[...].astype(F32), axis=0).astype(w_all.dtype)
        for to in row_peers:
            remote(w_all.at[side, row], w_all.at[side, row], wa_send, wa_recv, to, rep).start()

    def w_swap():
        side = rep % 2
        arrived = w_all.at[side, pl.ds(0, n_rows - 1)]
        remote(arrived, arrived, wa_send, wa_recv, row_peers[0], rep).wait_recv()
        post(w_all.at[side], w_all.at[side], swap_send, swap_recv, row, (rep + 1) % n_rep)

    def w_finish():
        other_side = w_all.at[(rep + 1) % 2]
        remote(other_side, other_side, swap_send, swap_recv, row, (rep + 1) % n_rep).wait_recv()
        whole = w_all[...].astype(F32)
        scale = lax.rsqrt(jnp.sum(whole * whole) / (width * width) + 1e-06)
        for side in range(2):
            for b in range(n_rows):
                wstep_ref[b * piece:(b + 1) * piece, side * half:(side + 1) * half] = whole[side, b] * scale

    def plane_product(o):
        place = pl.multiple_of(o * plane_nodes, plane_nodes)
        value = jnp.dot(dense_t[pl.ds(place, plane_nodes), :], row_grads, preferred_element_type=F32)
        return value.reshape(INNER, nodes, width)

    def give(src, dst, recv, row_to):
        remote(src, dst, rs_send, recv, row_to, rep).start()

    def taken(dst, recv):
        remote(dst, dst, rs_send, recv, at(outer, inner_x), rep).wait_recv()

    def far_terms(o):
        terms[plane_of(o)] = plane_product(o).astype(BF16)
        slot = other_slot(o, outer)
        for h in range(2):
            for n, i in enumerate(plane_inners):
                give(
                    terms.at[at(o, i), halves[h]], in_far.at[slot, h, n], in_far_recv.at[slot, h], at(outer, i),
                )

    def partner_terms():
        terms[plane_of(partner)] = plane_product(partner).astype(BF16)
        for n, i in enumerate(plane_inners + (inner,)):
            for h in range(2):
                give(
                    terms.at[at(partner, i), halves[h]], in_part.at[n, halves[h]],
                    in_part_recv.at[n, h], at(partner, inner),
                )

    def plane_sum(n):
        i = plane_inners[n]
        c = at(outer, i)
        for rows_at, recv in ((halves[0], in_part_recv.at[n, 0]), (halves[1], in_part_recv.at[n, 1])):
            taken(in_part.at[n, rows_at], recv)
            terms[c, rows_at] = (own_plane[i, rows_at] + in_part[n, rows_at].astype(F32)).astype(BF16)
            give(terms.at[c, rows_at], in_own.at[n, rows_at], in_own_recv, c)

    def far_sum(o):
        c, slot = at(o, inner), other_slot(o, outer)
        for h in range(2):
            taken(in_far.at[slot, h], in_far_recv.at[slot, h])
            total = terms[c, halves[h]].astype(F32)
            for n in range(INNER - 1):
                total = total + in_far[slot, h, n].astype(F32)
            terms[c, halves[h]] = total.astype(BF16)
            give(terms.at[c, halves[h]], in_z.at[other_slot(outer, o), halves[h]], in_z_recv, c)

    w_send_terms()
    for n, o in enumerate(far_reduce):
        far_terms(o)
        if n == 0:
            partner_terms()
    if not far_reduce:
        partner_terms()
    own_plane[...] = plane_product(outer)
    plane_sum(0)
    w_send_sums()
    for n, o in enumerate(far_reduce):
        far_sum(o)
        if n == 0:
            plane_sum(1)
            plane_sum(2)
    drain()
    sent = panel.at[pl.ds(0, n_rows - 1)]
    remote(sent, sent, ag_send, partner_recv, row_peers[0], rep).wait_send()
    for h in range(2):
        taken(in_part.at[INNER - 1, halves[h]], in_part_recv.at[INNER - 1, h])
    total = own_plane[inner] + in_part[INNER - 1].astype(F32)
    w_swap()
    taken(in_own, in_own_recv)
    for n in range(INNER - 1):
        total = total + in_own[n].astype(F32)
    w_finish()
    if far_reduce:
        taken(in_z, in_z_recv)
        for n in range(outer_count - 2):
            total = total + in_z[n].astype(F32)
    fgrad_ref[...] = total.astype(BF16)
    for source, send in (
        (terms.at[pl.ds(0, n_rows - 1)], rs_send), (w_out.at[pl.ds(0, n_rows - 1)], w_send),
        (w_all.at[0, pl.ds(0, n_rows - 1)], wa_send),
    ):
        remote(source, source, send, partner_recv, row_peers[0], rep).wait_send()
    drain()


def result_kernel(act_ref, fgrad_ref, wstep_ref, act_hbm, fgrad_hbm, wstep_hbm, sems):
    copies = [
        pltpu.make_async_copy(src, dst, sems.at[n])
        for n, (src, dst) in enumerate([(act_ref, act_hbm), (fgrad_ref, fgrad_hbm), (wstep_ref, wstep_hbm)])
    ]
    for copy in copies:
        copy.start()
    for copy in copies:
        copy.wait()


def body(n_rows, n_rep, features, weight, adj_tiles, tile_cols, tile_counts, out_grad, train_mask):
    nodes, width = features.shape
    tile_rows, tile = adj_tiles.shape[0], adj_tiles.shape[-1]
    others = max(n_rows // INNER - 2, 1)
    grads = (2, n_rep) if n_rep != 2 else (1, 1)
    piece = width // n_rows
    half = width // 2
    w_type = BF16 if piece % 16 == 0 else F32
    vmem = pl.BlockSpec(memory_space=pltpu.VMEM)
    hbm = pl.BlockSpec(memory_space=pltpu.HBM)
    dma = pltpu.SemaphoreType.DMA
    vmem_bytes = int((40 if n_rows <= 16 else 63) * 1024 * 1024)
    block = (nodes, width)
    outs = (
        jax.ShapeDtypeStruct(block, BF16),
        jax.ShapeDtypeStruct(block, BF16),
        jax.ShapeDtypeStruct((width, width), F32),
    )
    counts = tile_counts.reshape(-1)
    results = pl.pallas_call(
        functools.partial(layer_kernel, n_rows, n_rep),
        out_shape=tuple(pltpu.VMEM(out.shape, out.dtype) for out in outs),
        in_specs=[hbm] * 7,
        out_specs=(vmem, vmem, vmem),
        scratch_shapes=[
            pltpu.SMEM(tile_cols.shape, jnp.int32),
            pltpu.SMEM(counts.shape, jnp.int32),
            pltpu.VMEM(weight.shape, BF16),
            pltpu.VMEM(adj_tiles.shape, BF16),
            pltpu.VMEM(block, BF16),
            pltpu.VMEM((1, nodes), jnp.int32),
            pltpu.VMEM((n_rows,) + block, BF16),
            pltpu.VMEM((tile_rows * tile, n_rows * tile), BF16),
            pltpu.VMEM((n_rows * tile, tile_rows * tile), BF16),
            pltpu.VMEM((n_rep,) + block, BF16),
            pltpu.VMEM((n_rep * nodes, width), F32),
            pltpu.VMEM((n_rep,) + block, F32),
            pltpu.VMEM((2, n_rep) + block, BF16),
            pltpu.VMEM((width, width), F32),
            pltpu.VMEM((n_rows, piece, half), w_type),
            pltpu.VMEM((n_rows, piece, half), w_type),
            pltpu.VMEM((2, n_rows, piece, half), w_type),
            pltpu.VMEM((n_rows,) + block, BF16),
            pltpu.VMEM((INNER,) + block, F32),
            pltpu.VMEM((INNER,) + block, BF16),
            pltpu.VMEM((others, 2, INNER - 1, nodes // 2, width), BF16),
            pltpu.VMEM((INNER - 1,) + block, BF16),
            pltpu.VMEM((others,) + block, BF16),
            dma((7,)),
            dma, dma((INNER - 1, 2)), dma((others, 2)), dma((others,)), dma,
            dma, dma,
            dma((n_rep,)), dma((n_rep,)),
            dma(grads), dma(grads),
            dma, dma, dma, dma,
            dma, dma,
            dma, dma((INNER, 2)), dma((others, 2)), dma, dma,
        ],
        compiler_params=pltpu.CompilerParams(
            collective_id=0, has_side_effects=True, vmem_limit_bytes=vmem_bytes
        ),
    )(*[
        pltpu.with_memory_space_constraint(operand, pltpu.HBM)
        for operand in (features, weight, adj_tiles, tile_cols, counts, out_grad, train_mask.reshape(1, -1))
    ])
    return pl.pallas_call(
        result_kernel,
        out_shape=outs,
        in_specs=[vmem] * 3,
        out_specs=(hbm, hbm, hbm),
        scratch_shapes=[dma((3,))],
        compiler_params=pltpu.CompilerParams(vmem_limit_bytes=256 * 1024),
    )(*[pltpu.with_memory_space_constraint(result, pltpu.VMEM) for result in results])


def solution(mesh):
    placed = (
        P(("rows", "rep"), None),
        P(),
        P("rows", "rep", None, None, None),
        P("rows", "rep", None),
        P("rows", "rep"),
        P(("rows", "rep"), None),
        P(("rows", "rep")),
    )
    return jax.shard_map(
        functools.partial(body, mesh.shape["rows"], mesh.shape["rep"]),
        mesh=mesh,
        in_specs=placed,
        out_specs=(P(("rows", "rep"), None), P(("rows", "rep"), None), P()),
        check_vma=False,
    )
```

```python
import functools

import jax
import jax.numpy as jnp
from jax import lax
from jax.experimental import pallas as pl
from jax.experimental.pallas import tpu as pltpu
from jax.sharding import PartitionSpec as P

MESH = pl.DeviceIdType.MESH
F32 = jnp.float32
BF16 = jnp.bfloat16
INNER = 4


def layer_kernel(
    n_rows, n_rep,
    feat_hbm, weight_hbm, adj_hbm, cols_hbm, counts_hbm, grad_hbm, mask_hbm,
    act_ref, fgrad_ref, wstep_ref,
    cols_ref, counts_ref, weight_ref, adj_ref, grad_ref, mask_ref,
    panel, dense, dense_t, masked, acc, part_in, shared,
    w_full, w_out, w_in, w_all, terms, own_plane, in_part, in_far, in_own, in_z,
    load_sem, ag_send, own_recv, far_recv, plane_recv, partner_recv, masked_send, masked_recv,
    part_send, part_recv, grads_send, grads_recv, w_send, w_recv, wa_send, wa_recv, swap_send, swap_recv,
    rs_send, in_part_recv, in_far_recv, in_own_recv, in_z_recv,
):
    nodes, width = feat_hbm.shape
    tile_rows, slots, tile = adj_ref.shape[0], adj_ref.shape[2], adj_ref.shape[3]
    piece = w_out.shape[1]
    half = w_out.shape[2]
    outer_count = n_rows // INNER
    both = n_rep == 2
    block_rows = n_rep * nodes
    plane_nodes = INNER * nodes
    row = lax.axis_index("rows")
    rep = lax.axis_index("rep")
    outer, inner = row // INNER, row % INNER
    iy, ix = inner // 2, inner % 2
    inner_x, inner_y = iy * 2 + (1 - ix), (1 - iy) * 2 + ix
    inner_d = (1 - iy) * 2 + (1 - ix)
    side_of = outer % 2
    partner = outer + 1 - 2 * side_of
    pair, pairs = outer // 2, outer_count // 2
    others = [(pair + d) % pairs for d in range(1, pairs)]
    far_gather = [2 * q + m for q in others for m in (1 - side_of, side_of)]
    far_reduce = [2 * q + m for q in others[::-1] for m in (side_of, 1 - side_of)]
    rep_peers = [(rep + d) % n_rep for d in range(1, n_rep)]
    row_peers = [(row + d) % n_rows for d in range(1, n_rows)]
    plane_inners = (inner_d, inner_x, inner_y)
    halves = [pl.ds(h * (nodes // 2), nodes // 2) for h in range(2)]
    pending = []
    smooth = {}

    def remote(src, dst, send, recv, row_to, rep_to):
        return pltpu.make_async_remote_copy(
            src_ref=src, dst_ref=dst, send_sem=send, recv_sem=recv,
            device_id=(row_to, rep_to), device_id_type=MESH,
        )

    def post(*spec):
        copy = remote(*spec)
        copy.start()
        pending.append(copy)

    def drain():
        while pending:
            pending.pop(0).wait_send()

    def at(o, i):
        return o * INNER + i

    def other_slot(o, seen_from):
        return ((o // 2 - seen_from // 2 + pairs) % pairs - 1) * 2 + o % 2

    def plane_of(o, count=INNER):
        return pl.ds(pl.multiple_of(o * INNER, INNER), count)

    barrier = pltpu.get_barrier_semaphore()
    near = [(at(o, inner), rep) for o in [partner] + far_gather]
    near += [(at(outer, i), rep) for i in plane_inners]
    near += [(row, p) for p in rep_peers]
    loads = [
        pltpu.make_async_copy(src, dst, load_sem.at[n])
        for n, (src, dst) in enumerate([
            (adj_hbm, adj_ref), (cols_hbm, cols_ref), (counts_hbm, counts_ref),
            (grad_hbm, grad_ref), (mask_hbm, mask_ref), (weight_hbm, weight_ref), (feat_hbm, panel.at[row]),
        ])
    ]
    loads[-1].start()
    for other in near:
        pl.semaphore_signal(barrier, inc=1, device_id=other, device_id_type=MESH)
    for load in loads[:-1]:
        load.start()
    pl.semaphore_wait(barrier, len(near))
    loads[-1].wait()

    def gather(src, source, row_to, recv):
        for h in range(2):
            remote(src.at[halves[h]], panel.at[source, halves[h]], ag_send, recv[h], row_to, rep).start()

    def gathered(blocks, recv):
        remote(panel.at[blocks], panel.at[blocks], ag_send, recv, at(outer, inner_x), rep).wait_recv()

    for o in far_gather:
        gather(panel.at[row], row, at(o, inner), [far_recv.at[other_slot(outer, o), h] for h in range(2)])
    for n, i in enumerate(plane_inners):
        gather(panel.at[row], row, at(outer, i), [own_recv.at[n, h] for h in range(2)])
    gather(panel.at[row], row, at(partner, inner), [partner_recv] * 2)
    for load in loads[:5]:
        load.wait()

    def build(r, start, stop):
        def column(c, carry):
            total = jnp.zeros((tile, tile), F32)
            for k in range(slots):
                chosen = jnp.logical_and(cols_ref[r, 0, k] == c, k < counts_ref[r])
                total = total + jnp.where(chosen, 1.0, 0.0) * adj_ref[r, 0, k].astype(F32)
            place = pl.multiple_of(c * tile, tile)
            dense[r * tile:(r + 1) * tile, pl.ds(place, tile)] = total.astype(BF16)
            dense_t[pl.ds(place, tile), r * tile:(r + 1) * tile] = total.T.astype(BF16)
            return carry

        lax.fori_loop(start, stop, column, 0)

    stride = n_rows // 8
    jobs = [(r, c, c + stride) for r in range(tile_rows) for c in range(0, n_rows, stride)]

    def build_jobs(count):
        for _ in range(min(count, len(jobs))):
            build(*jobs.pop(0))

    mask_col = jnp.broadcast_to(mask_ref[...].astype(F32), (nodes, nodes)).T
    mask = jnp.concatenate([mask_col] * (width // nodes), axis=1)
    masked[rep] = (grad_ref[...].astype(F32) * mask).astype(BF16)
    if both:
        for p in rep_peers:
            post(masked.at[rep], masked.at[rep], masked_send, masked_recv, row, p)

    def pass_on(source, recvs, targets, recv):
        for h in range(2):
            half_block = panel.at[source, halves[h]]
            remote(half_block, half_block, ag_send, recvs.at[h], at(outer, inner_x), rep).wait_recv()
            for to in targets:
                remote(half_block, half_block, ag_send, recv, to, rep).start()

    def to_partner(n):
        pass_on(at(outer, plane_inners[n]), own_recv.at[n], [at(partner, inner)], partner_recv)

    def to_plane(o):
        slot = other_slot(o, outer)
        pass_on(at(o, inner), far_recv.at[slot], [at(outer, i) for i in plane_inners], plane_recv.at[slot])

    share = len(jobs)
    build_jobs(share // 4)
    to_partner(1)
    to_partner(2)
    for n, o in enumerate(far_gather):
        if n > 0:
            build_jobs(max(1, share // (8 * (len(far_gather) - 1))))
        to_plane(o)
        if n == 0:
            to_partner(0)
    build_jobs(len(jobs))
    loads[5].wait()

    def product(o, rows_at):
        place = pl.multiple_of(o * plane_nodes, plane_nodes)
        planes = panel[plane_of(o)].reshape(plane_nodes, width)
        return jnp.dot(dense[rows_at, pl.ds(place, plane_nodes)], planes, preferred_element_type=F32)

    everything = pl.ds(0, block_rows)
    order = [outer] + far_gather[:-1] + [partner] + far_gather[-1:]
    for n, o in enumerate(order[:-1]):
        if n == len(order) - 2 or not far_gather:
            gathered(plane_of(partner), partner_recv)
        elif n > 0:
            gathered(plane_of(o, INNER - 1), plane_recv.at[other_slot(o, outer)])
        value = product(o, everything)
        acc[...] = value if n == 0 else acc[...] + value
    last = order[-1]
    if far_gather:
        gathered(plane_of(last, INNER - 1), plane_recv.at[other_slot(last, outer)])

    def rows_of(p):
        return pl.ds(p * nodes if isinstance(p, int) else pl.multiple_of(p * nodes, nodes), nodes)

    def finish_product(p):
        acc[rows_of(p), :] = acc[rows_of(p), :] + product(last, rows_of(p))

    def slope_of(pre_act, sigmoid):
        return sigmoid * (1.0 + pre_act * (1.0 - sigmoid))

    if both:
        other = rep_peers[0]
        for r in range(n_rep):
            finish_product(r)
            post(acc.at[rows_of(r)], part_in.at[r], part_send.at[r], part_recv.at[r], row, other)
        remote(masked.at[rep], masked.at[other], masked_send, masked_recv, row, other).wait_recv()
        for r in range(n_rep):
            remote(acc.at[rows_of(r)], part_in.at[r], part_send.at[r], part_recv.at[r], row, other).wait_recv()
            aggregated = (acc[rows_of(r), :] + part_in[r]).astype(BF16)
            shared[0, r] = aggregated
            pre_act = jnp.dot(aggregated, weight_ref[...], preferred_element_type=F32)
            sigmoid = jax.nn.sigmoid(pre_act)
            pre_grad = (masked[r].astype(F32) * slope_of(pre_act, sigmoid)).astype(BF16)
            shared[1, r] = pre_grad
            term = lax.dot_general(aggregated, pre_grad, (((0,), (0,)), ((), ())), preferred_element_type=F32)
            w_full[...] = term if r == 0 else w_full[...] + term

            smooth[r] = (pre_act * sigmoid).astype(BF16)
    else:
        for d, p in enumerate(rep_peers):
            finish_product(p)
            post(acc.at[rows_of(p)], part_in.at[rep], part_send.at[d], part_recv.at[rep], row, p)
        finish_product(rep)
        total = acc[rows_of(rep), :]
        for p in rep_peers:
            remote(acc.at[rows_of(p)], part_in.at[p], part_send.at[0], part_recv.at[p], row, p).wait_recv()
            total = total + part_in[p]
        aggregated = total.astype(BF16)
        shared[0, rep] = aggregated
        for d, p in enumerate(rep_peers):
            post(shared.at[0, rep], shared.at[0, rep], grads_send.at[0, d], grads_recv.at[0, rep], row, p)
        pre_act = jnp.dot(aggregated, weight_ref[...], preferred_element_type=F32)
        sigmoid = jax.nn.sigmoid(pre_act)
        shared[1, rep] = (masked[rep].astype(F32) * slope_of(pre_act, sigmoid)).astype(BF16)
        for d, p in enumerate(rep_peers):
            post(shared.at[1, rep], shared.at[1, rep], grads_send.at[1, d], grads_recv.at[1, rep], row, p)
        act_ref[...] = (pre_act * sigmoid).astype(BF16)
        for n in range(2):
            for p in rep_peers:
                remote(shared.at[n, p], shared.at[n, p], grads_send.at[0, 0], grads_recv.at[n, p], row, p).wait_recv()

    row_pre_grads = shared[1].reshape(block_rows, width)
    row_grads = lax.dot_general(
        row_pre_grads, weight_ref[...], (((1,), (1,)), ((), ())), preferred_element_type=F32
    ).astype(BF16)

    def w_send_terms():
        column = pl.multiple_of((rep % 2) * half, half)
        if not both:
            w_full[...] = lax.dot_general(
                shared[0].reshape(block_rows, width), row_pre_grads,
                (((0,), (0,)), ((), ())), preferred_element_type=F32,
            )
        w_half = w_full[:, pl.ds(column, half)]
        for b in range(n_rows):
            w_out[b] = w_half[b * piece:(b + 1) * piece].astype(w_out.dtype)
        for to in row_peers:
            remote(w_out.at[to], w_in.at[row], w_send, w_recv, to, rep).start()
        w_in[row] = w_out[row]

    def w_send_sums():
        arrived = w_in.at[pl.ds(0, n_rows - 1)]
        remote(arrived, arrived, w_send, w_recv, row_peers[0], rep).wait_recv()
        side = rep % 2
        w_all[side, row] = jnp.sum(w_in[...].astype(F32), axis=0).astype(w_all.dtype)
        for to in row_peers:
            remote(w_all.at[side, row], w_all.at[side, row], wa_send, wa_recv, to, rep).start()

    def w_swap():
        side = rep % 2
        arrived = w_all.at[side, pl.ds(0, n_rows - 1)]
        remote(arrived, arrived, wa_send, wa_recv, row_peers[0], rep).wait_recv()
        post(w_all.at[side], w_all.at[side], swap_send, swap_recv, row, (rep + 1) % n_rep)

    def w_finish():
        mine = w_all[rep % 2].astype(F32)
        squares = jnp.sum(mine * mine)
        other_side = w_all.at[(rep + 1) % 2]
        remote(other_side, other_side, swap_send, swap_recv, row, (rep + 1) % n_rep).wait_recv()
        given = w_all[(rep + 1) % 2].astype(F32)
        scale = lax.rsqrt((squares + jnp.sum(given * given)) / (width * width) + 1e-06)
        whole = w_all[...].astype(F32)
        for side in range(2):
            for b in range(n_rows):
                wstep_ref[b * piece:(b + 1) * piece, side * half:(side + 1) * half] = whole[side, b] * scale

    def plane_product(o):
        place = pl.multiple_of(o * plane_nodes, plane_nodes)
        value = jnp.dot(dense_t[pl.ds(place, plane_nodes), :], row_grads, preferred_element_type=F32)
        return value.reshape(INNER, nodes, width)

    def give(src, dst, recv, row_to):
        remote(src, dst, rs_send, recv, row_to, rep).start()

    def taken(dst, recv):
        remote(dst, dst, rs_send, recv, at(outer, inner_x), rep).wait_recv()

    def far_terms(o):
        terms[plane_of(o)] = plane_product(o).astype(BF16)
        slot = other_slot(o, outer)
        for h in range(2):
            for n, i in enumerate(plane_inners):
                give(
                    terms.at[at(o, i), halves[h]], in_far.at[slot, h, n], in_far_recv.at[slot, h], at(outer, i),
                )

    def partner_terms():
        terms[plane_of(partner)] = plane_product(partner).astype(BF16)
        for n, i in enumerate(plane_inners):
            partner_term(n, i)

    def partner_term(n, i):
        for h in range(2):
            give(
                terms.at[at(partner, i), halves[h]], in_part.at[n, halves[h]],
                in_part_recv.at[n, h], at(partner, inner),
            )

    def plane_sum(n):
        i = plane_inners[n]
        c = at(outer, i)
        for rows_at, recv in ((halves[0], in_part_recv.at[n, 0]), (halves[1], in_part_recv.at[n, 1])):
            taken(in_part.at[n, rows_at], recv)
            terms[c, rows_at] = (own_plane[i, rows_at] + in_part[n, rows_at].astype(F32)).astype(BF16)
            give(terms.at[c, rows_at], in_own.at[n, rows_at], in_own_recv, c)

    def far_sum(o):
        c, slot = at(o, inner), other_slot(o, outer)
        for h in range(2):
            taken(in_far.at[slot, h], in_far_recv.at[slot, h])
            total = terms[c, halves[h]].astype(F32)
            for n in range(INNER - 1):
                total = total + in_far[slot, h, n].astype(F32)
            terms[c, halves[h]] = total.astype(BF16)
            give(terms.at[c, halves[h]], in_z.at[other_slot(outer, o), halves[h]], in_z_recv, c)

    w_send_terms()
    for n, o in enumerate(far_reduce):
        far_terms(o)
        if n == 0:
            partner_terms()
    if not far_reduce:
        partner_terms()
    own_plane[...] = plane_product(outer)
    for r, value in smooth.items():
        @pl.when(rep == r)
        def _():
            act_ref[...] = value

    plane_sum(0)
    partner_term(INNER - 1, inner)
    w_send_sums()
    for n, o in enumerate(far_reduce):
        far_sum(o)
        if n == 0:
            plane_sum(1)
            plane_sum(2)
    drain()
    sent = panel.at[pl.ds(0, n_rows - 1)]
    remote(sent, sent, ag_send, partner_recv, row_peers[0], rep).wait_send()
    for h in range(2):
        taken(in_part.at[INNER - 1, halves[h]], in_part_recv.at[INNER - 1, h])
    total = own_plane[inner] + in_part[INNER - 1].astype(F32)
    w_swap()
    taken(in_own, in_own_recv)
    for n in range(INNER - 1):
        total = total + in_own[n].astype(F32)
    w_finish()
    if far_reduce:
        taken(in_z, in_z_recv)
        for n in range(outer_count - 2):
            total = total + in_z[n].astype(F32)
    fgrad_ref[...] = total.astype(BF16)
    for source, send in (
        (terms.at[pl.ds(0, n_rows - 1)], rs_send), (w_out.at[pl.ds(0, n_rows - 1)], w_send),
        (w_all.at[0, pl.ds(0, n_rows - 1)], wa_send),
    ):
        remote(source, source, send, partner_recv, row_peers[0], rep).wait_send()
    drain()


def result_kernel(act_ref, fgrad_ref, wstep_ref, act_hbm, fgrad_hbm, wstep_hbm, sems):
    copies = [
        pltpu.make_async_copy(src, dst, sems.at[n])
        for n, (src, dst) in enumerate([(act_ref, act_hbm), (fgrad_ref, fgrad_hbm), (wstep_ref, wstep_hbm)])
    ]
    for copy in copies:
        copy.start()
    for copy in copies:
        copy.wait()


def body(n_rows, n_rep, features, weight, adj_tiles, tile_cols, tile_counts, out_grad, train_mask):
    nodes, width = features.shape
    tile_rows, tile = adj_tiles.shape[0], adj_tiles.shape[-1]
    others = max(n_rows // INNER - 2, 1)
    grads = (2, n_rep) if n_rep != 2 else (1, 1)
    piece = width // n_rows
    half = width // 2
    w_type = BF16 if piece % 16 == 0 else F32
    vmem = pl.BlockSpec(memory_space=pltpu.VMEM)
    hbm = pl.BlockSpec(memory_space=pltpu.HBM)
    dma = pltpu.SemaphoreType.DMA
    vmem_bytes = int((40 if n_rows <= 16 else 63) * 1024 * 1024)
    block = (nodes, width)
    outs = (
        jax.ShapeDtypeStruct(block, BF16),
        jax.ShapeDtypeStruct(block, BF16),
        jax.ShapeDtypeStruct((width, width), F32),
    )
    counts = tile_counts.reshape(-1)
    results = pl.pallas_call(
        functools.partial(layer_kernel, n_rows, n_rep),
        out_shape=tuple(pltpu.VMEM(out.shape, out.dtype) for out in outs),
        in_specs=[hbm] * 7,
        out_specs=(vmem, vmem, vmem),
        scratch_shapes=[
            pltpu.SMEM(tile_cols.shape, jnp.int32),
            pltpu.SMEM(counts.shape, jnp.int32),
            pltpu.VMEM(weight.shape, BF16),
            pltpu.VMEM(adj_tiles.shape, BF16),
            pltpu.VMEM(block, BF16),
            pltpu.VMEM((1, nodes), jnp.int32),
            pltpu.VMEM((n_rows,) + block, BF16),
            pltpu.VMEM((tile_rows * tile, n_rows * tile), BF16),
            pltpu.VMEM((n_rows * tile, tile_rows * tile), BF16),
            pltpu.VMEM((n_rep,) + block, BF16),
            pltpu.VMEM((n_rep * nodes, width), F32),
            pltpu.VMEM((n_rep,) + block, F32),
            pltpu.VMEM((2, n_rep) + block, BF16),
            pltpu.VMEM((width, width), F32),
            pltpu.VMEM((n_rows, piece, half), w_type),
            pltpu.VMEM((n_rows, piece, half), w_type),
            pltpu.VMEM((2, n_rows, piece, half), w_type),
            pltpu.VMEM((n_rows,) + block, BF16),
            pltpu.VMEM((INNER,) + block, F32),
            pltpu.VMEM((INNER,) + block, BF16),
            pltpu.VMEM((others, 2, INNER - 1, nodes // 2, width), BF16),
            pltpu.VMEM((INNER - 1,) + block, BF16),
            pltpu.VMEM((others,) + block, BF16),
            dma((7,)),
            dma, dma((INNER - 1, 2)), dma((others, 2)), dma((others,)), dma,
            dma, dma,
            dma((n_rep,)), dma((n_rep,)),
            dma(grads), dma(grads),
            dma, dma, dma, dma,
            dma, dma,
            dma, dma((INNER, 2)), dma((others, 2)), dma, dma,
        ],
        compiler_params=pltpu.CompilerParams(
            collective_id=0, has_side_effects=True, vmem_limit_bytes=vmem_bytes
        ),
    )(*[
        pltpu.with_memory_space_constraint(operand, pltpu.HBM)
        for operand in (features, weight, adj_tiles, tile_cols, counts, out_grad, train_mask.reshape(1, -1))
    ])
    return pl.pallas_call(
        result_kernel,
        out_shape=outs,
        in_specs=[vmem] * 3,
        out_specs=(hbm, hbm, hbm),
        scratch_shapes=[dma((3,))],
        compiler_params=pltpu.CompilerParams(vmem_limit_bytes=256 * 1024),
    )(*[pltpu.with_memory_space_constraint(result, pltpu.VMEM) for result in results])


def solution(mesh):
    placed = (
        P(("rows", "rep"), None),
        P(),
        P("rows", "rep", None, None, None),
        P("rows", "rep", None),
        P("rows", "rep"),
        P(("rows", "rep"), None),
        P(("rows", "rep")),
    )
    return jax.shard_map(
        functools.partial(body, mesh.shape["rows"], mesh.shape["rep"]),
        mesh=mesh,
        in_specs=placed,
        out_specs=(P(("rows", "rep"), None), P(("rows", "rep"), None), P()),
        check_vma=False,
    )
```
